32 devices in a mesh: lat: 4 (over x, core), lon: 8 (over z, y).
Axes of the slice: x: 2, y: 2, z: 4, core: 2. Of those that a mesh axis runs over, the one named last changes fastest.
Arguments:
- ensemble: bfloat16 [80, 8, 32, 1024], P(None, None, 'lat', 'lon'), may hold values from -6 to 6
- static_sigma: float32 [8], replicated, may hold values from 0.5 to 2
- lat_taps: float32 [17], replicated, may hold values from 0.01 to 0.12
- lon_taps: float32 [17], replicated, may hold values from 0.01 to 0.12
- step_len: float32 [2], replicated, may hold values from 0.2 to 0.6
- send_cols: int32 [4, 8, 32, 256], P('lat', 'lon'), may hold values from 0 to 1023
- send_count: int32 [4, 8, 32], P('lat', 'lon'), may hold values from 128 to 256, as said below
- obs_ref: int32 [4, 8, 4, 2048], P('lat', 'lon'), may hold values from 0 to 8191, as said below
- obs_level: int32 [4, 8, 2048], P('lat', 'lon'), may hold values from 0 to 7
- obs_weight: float32 [4, 8, 4, 2048], P('lat', 'lon'), may hold values from 0 to 1
- innovation: float32 [4, 8, 2048], P('lat', 'lon'), may hold values from -6 to 6
- obs_precision: float32 [4, 8, 2048], P('lat', 'lon'), may hold values from 0.25 to 1
Outputs:
- ens_control: float32 [80, 8, 32, 1024], P(None, None, 'lat', 'lon')
- static_control: float32 [8, 32, 1024], P(None, 'lat', 'lon')
- departures: float32 [4, 8, 2048], P('lat', 'lon')
The draws below stay inside these ranges and needn't reach their ends.
Inputs may be any that keep to these rules, and one draw needn't show every extreme that they name: `send_count`: number of leading slots of send_cols[a, b, e] that are live. One device receives 256 live slots from every device. `obs_ref`: position in the owning device's list L_e of received live columns; always below the total live slots that device receives.
All inputs are finite; a program needn't handle non-finite values.
Results may differ from the reference program's by a relative error of at most 0.0003.
Values may be sent and summed in bfloat16 or wider, within the bound.
A program may use at most 128 MiB of HBM per device.

```python
import math
import jax
import jax.numpy as jnp
from jax import lax

MEM = 80
LEV = 8
HW = 8
ITERS = 2
CLAT = 8
CLON = 128
NOBS_DEV = 2048
SLOT = 256
NLAT = 32
NLON = 1024
N_LAT = 4
N_LON = 8
DEVICES = 32


def count_table(key):
    table_key = jax.random.fold_in(key, 11)
    lead_key, hot_key = jax.random.split(table_key, 2)
    base_count = jax.random.randint(lead_key, (N_LAT, N_LON, DEVICES), SLOT // 2, SLOT + 1)
    hot_target = jax.random.randint(hot_key, (), 0, DEVICES)
    target = lax.broadcasted_iota(jnp.int32, (N_LAT, N_LON, DEVICES), 2)
    return jnp.where(target == hot_target, SLOT, base_count).astype(jnp.int32)


def draw_send_count(key, part):
    return count_table(key)


def draw_obs_ref(key, part):
    counts = count_table(key).reshape(DEVICES, DEVICES)
    totals = jnp.sum(counts, axis=0).reshape(N_LAT, N_LON, 1, 1)
    raw_draw = jax.random.randint(jax.random.fold_in(key, 23), (N_LAT, N_LON, 4, NOBS_DEV), 0, 2 ** 30)
    return (raw_draw % totals).astype(jnp.int32)


def place_ends(entries, stream_key, low, top_value):
    dims = entries.shape
    index_at = [jax.random.randint(jax.random.fold_in(stream_key, axis), (), 0, dims[axis]) for axis in range(len(dims))]
    entries = entries.at[tuple(index_at)].set(low)
    longest = dims.index(max(dims))
    index_at[longest] = (index_at[longest] + 1) % dims[longest]
    return entries.at[tuple(index_at)].set(top_value)


def shard_levels(stream_key, extent, cuts, smallest, top_value):
    def one(position, blocks):
        draws = jax.random.uniform(jax.random.fold_in(jax.random.fold_in(stream_key, 6), position), (blocks,), jnp.float32, smallest / len(cuts), top_value / len(cuts))
        return jnp.repeat(jnp.exp(draws), extent[position] // blocks).reshape((-1,) + (1,) * (len(extent) - position - 1))

    factor_of = one(*cuts[0])
    for cut in cuts[1:]:
        factor_of = factor_of * one(*cut)
    return factor_of


def scatter_about(stream_key, shape, width, bound, cuts=(), kind=jnp.bfloat16):
    values = width * jax.random.normal(stream_key, shape, jnp.float32)
    if cuts:
        values = values * shard_levels(stream_key, shape, cuts, -0.22, 0.18)
    return jnp.clip(values, -bound, bound).astype(kind)


def setup_inputs(seed: int = 0) -> dict:
    streams_of = jax.random.split(jax.random.key(seed), 13)
    ensemble = scatter_about(streams_of[0], (MEM, LEV, NLAT, NLON), 1.0, 6.0, ((2, 4), (3, 8)))
    static_sigma = jnp.clip(jnp.exp(jax.random.uniform(streams_of[1], (LEV,), jnp.float32, math.log(0.5), math.log(2.0))), 0.5, 2.0)
    lat_taps = jnp.clip(jnp.exp(jax.random.uniform(streams_of[2], (2 * HW + 1,), jnp.float32, math.log(0.01), math.log(0.12))), 0.01, 0.12)
    lon_taps = jnp.clip(jnp.exp(jax.random.uniform(streams_of[3], (2 * HW + 1,), jnp.float32, math.log(0.01), math.log(0.12))), 0.01, 0.12)
    step_len = jnp.clip(jax.random.uniform(streams_of[4], (ITERS,), jnp.float32, 0.2, 0.6), 0.2, 0.6)
    send_cols = place_ends(jax.random.randint(streams_of[5], (N_LAT, N_LON, DEVICES, SLOT), 0, CLAT * CLON), jax.random.fold_in(streams_of[5], 1), 0, (CLAT * CLON) - 1).astype(jnp.int32)
    send_count = draw_send_count(jax.random.fold_in(streams_of[12], 71), 0)
    obs_ref = draw_obs_ref(jax.random.fold_in(streams_of[12], 71), 0)
    obs_level = place_ends(jax.random.randint(streams_of[8], (N_LAT, N_LON, NOBS_DEV), 0, LEV), jax.random.fold_in(streams_of[8], 1), 0, LEV - 1).astype(jnp.int32)
    obs_weight = jnp.clip(1.0 * jax.random.uniform(streams_of[9], (N_LAT, N_LON, 4, NOBS_DEV), jnp.float32) ** shard_levels(streams_of[9], (N_LAT, N_LON, 4, NOBS_DEV), ((0, 4), (1, 8)), -0.2, 0.2), 0.0, 1.0)
    innovation = scatter_about(streams_of[10], (N_LAT, N_LON, NOBS_DEV), 1.0, 6.0, ((0, 4), (1, 8)), jnp.float32)
    obs_precision = jnp.clip(jnp.exp(math.log(1.0) - 1.3862944 * jax.random.uniform(streams_of[11], (N_LAT, N_LON, NOBS_DEV), jnp.float32) ** shard_levels(streams_of[11], (N_LAT, N_LON, NOBS_DEV), ((0, 4), (1, 8)), -0.2, 0.2)), 0.25, 1.0)
    return dict(ensemble=ensemble, static_sigma=static_sigma, lat_taps=lat_taps, lon_taps=lon_taps, step_len=step_len, send_cols=send_cols, send_count=send_count, obs_ref=obs_ref, obs_level=obs_level, obs_weight=obs_weight, innovation=innovation, obs_precision=obs_precision)


HYBRID_STATIC = 0.5
HYBRID_ENSEMBLE = 0.8660254037844386

def smooth_whole(fields, lat_taps, lon_taps):
    half_width = (lat_taps.shape[0] - 1) // 2
    lat_count = fields.shape[1]
    padded = jnp.pad(fields, ((0, 0), (half_width, half_width), (0, 0)))
    lat_pass = jnp.zeros_like(fields)
    for offset in range(2 * half_width + 1):
        lat_pass = lat_pass + lat_taps[offset] * padded[:, offset:offset + lat_count, :]
    result = jnp.zeros_like(fields)
    for offset in range(2 * half_width + 1):
        result = result + lon_taps[offset] * jnp.roll(lat_pass, half_width - offset, axis=2)
    return result

def smooth_adjoint(fields, lat_taps, lon_taps):
    half_width = (lat_taps.shape[0] - 1) // 2
    lat_count = fields.shape[1]
    lat_flip = lat_taps[::-1]
    lon_flip = lon_taps[::-1]
    lon_pass = jnp.zeros_like(fields)
    for offset in range(2 * half_width + 1):
        lon_pass = lon_pass + lon_flip[offset] * jnp.roll(fields, half_width - offset, axis=2)
    padded = jnp.pad(lon_pass, ((0, 0), (half_width, half_width), (0, 0)))
    result = jnp.zeros_like(fields)
    for offset in range(2 * half_width + 1):
        result = result + lat_flip[offset] * padded[:, offset:offset + lat_count, :]
    return result

def reference(ensemble, static_sigma, lat_taps, lon_taps, step_len, send_cols, send_count, obs_ref, obs_level, obs_weight, innovation, obs_precision):
    device_count = N_LAT * N_LON
    slot_count = send_cols.shape[-1]
    members, level_count, lat_total, lon_total = ensemble.shape
    lat_rows = lat_total // N_LAT
    lon_cells = lon_total // N_LON
    counts = send_count.reshape(device_count, device_count)
    slot_ends = jnp.cumsum(counts, axis=0)
    column_table = send_cols.reshape(device_count, device_count, slot_count)
    positions = obs_ref.reshape(device_count, 4, -1)

    def locate(target):
        target_ends = slot_ends[:, target]
        source = jnp.searchsorted(target_ends, positions[target], side='right').astype(jnp.int32)
        first_slot = (target_ends - counts[:, target])[source]
        local_cell = column_table[source, target, positions[target] - first_slot]
        grid_row = source // N_LON * lat_rows + local_cell // lon_cells
        grid_col = source % N_LON * lon_cells + local_cell % lon_cells
        return (grid_row, grid_col)
    grid_rows, grid_cols = jax.vmap(locate)(jnp.arange(device_count, dtype=jnp.int32))
    levels = jnp.broadcast_to(obs_level.reshape(device_count, 1, -1), grid_rows.shape)
    weights = obs_weight.reshape(device_count, 4, -1)
    innovations = innovation.reshape(device_count, -1)
    precision_obs = obs_precision.reshape(device_count, -1)
    ens_scale = HYBRID_ENSEMBLE / math.sqrt(members - 1)
    sigma = static_sigma[:, None, None]
    control = jnp.zeros(ensemble.shape, jnp.float32)
    static = jnp.zeros((level_count, lat_total, lon_total), jnp.float32)
    departure = -innovations
    for iteration in range(ITERS):
        if iteration > 0:

            def accumulate(running, member_pair):
                member, member_control = member_pair
                return (running + member.astype(jnp.float32) * smooth_whole(member_control, lat_taps, lon_taps), None)
            ens_part, unused = lax.scan(accumulate, jnp.zeros((level_count, lat_total, lon_total), jnp.float32), (ensemble, control))
            increment = ens_scale * ens_part + HYBRID_STATIC * sigma * smooth_whole(static, lat_taps, lon_taps)
            departure = lax.optimization_barrier(jnp.sum(weights * increment[levels, grid_rows, grid_cols], axis=1)) - innovations
        forcing = jnp.zeros((level_count, lat_total, lon_total), jnp.float32).at[levels, grid_rows, grid_cols].add(weights * (precision_obs * departure)[:, None, :])
        adjoint = lax.map(lambda member: smooth_adjoint(member.astype(jnp.float32) * forcing, lat_taps, lon_taps), ensemble)
        control = control - step_len[iteration] * (ens_scale * adjoint + control)
        static = static - step_len[iteration] * (HYBRID_STATIC * sigma * smooth_adjoint(forcing, lat_taps, lon_taps) + static)
    return (control, static, departure.reshape(N_LAT, N_LON, -1))
```

```python
import functools
import math

import jax
import jax.numpy as jnp
from jax import lax
from jax.experimental import pallas as pl
from jax.experimental.pallas import tpu as pltpu
from jax.sharding import PartitionSpec as P

HYBRID_STATIC = 0.5
HYBRID_ENSEMBLE = 0.8660254037844386
BF16 = jnp.bfloat16
F32 = jnp.float32
MESH = pl.DeviceIdType.MESH
CHUNKS = 4
VMEM_LIMIT = 40 * 2**20
VMEM = pl.BlockSpec(memory_space=pltpu.VMEM)


def halves(x):
    high = x.astype(BF16)
    return high, (x - high.astype(F32)).astype(BF16)


def dot(a, b):
    return jnp.dot(a, b, preferred_element_type=F32)


def dot_nt(a, b):
    return lax.dot_general(a, b, (((1,), (1,)), ((), ())), preferred_element_type=F32)


def dot3(a, b):
    a_high, a_low = halves(a)
    b_high, b_low = halves(b)
    return dot(a_high, b_high) + dot(a_high, b_low) + dot(a_low, b_high)


def iota(shape, dim):
    return lax.broadcasted_iota(jnp.int32, shape, dim)


def obs_step(table, hi, lo, weight, innov, prec, departure, out, rows, slots):
    chunk = 512 if rows <= 256 else 256
    points = hi.shape[0]
    if table is not None:
        table_high, table_low = halves(table[...].reshape(rows, slots))

    def step(index, carry):
        where = pl.ds(pl.multiple_of(index * chunk, chunk), chunk)
        row_ids = iota((rows, chunk), 0)
        slot_ids = iota((slots, chunk), 0)
        value = -innov[:, where]
        if table is not None:
            for q in range(points):
                lo_hot = jnp.where(slot_ids == lo[q : q + 1, where], 1.0, 0.0).astype(BF16)
                product = dot(table_high, lo_hot) + dot(table_low, lo_hot)
                picked = jnp.sum(
                    jnp.where(row_ids == hi[q : q + 1, where], product, 0.0), axis=0, keepdims=True
                )
                value = value + weight[q : q + 1, where] * picked
            departure[:, where] = value
        value = prec[:, where] * value
        total = None
        for q in range(points):
            lo_hot = jnp.where(slot_ids == lo[q : q + 1, where], 1.0, 0.0).astype(BF16)
            pushed = weight[q : q + 1, where] * value
            high = pushed.astype(BF16).astype(F32)
            chosen = row_ids == hi[q : q + 1, where]
            term = dot_nt(jnp.where(chosen, high, 0.0).astype(BF16), lo_hot) + dot_nt(
                jnp.where(chosen, pushed - high, 0.0).astype(BF16), lo_hot
            )
            total = term if total is None else total + term
        return carry + total

    total = lax.fori_loop(0, hi.shape[1] // chunk, step, jnp.zeros((rows, slots), F32))
    out[...] = total.reshape(out.shape)


def cell_and_row(col, cells):
    if cells & (cells - 1):
        return col % cells, col // cells
    return jnp.bitwise_and(col, cells - 1), jnp.right_shift(col, cells.bit_length() - 1)


def split(ids, size):
    inner, outer = cell_and_row(ids, size)
    return outer, inner


def to_slots(cols, field, out):
    levels, lat_rows, cells = field.shape
    slots = out.shape[2]
    width = cols.shape[1]
    per_row = width // slots
    rows = jnp.concatenate([field[:, r, :] for r in range(lat_rows)], axis=0)
    count = rows.shape[0]
    both = jnp.concatenate(halves(rows), axis=0)

    def step(index, carry):
        col = cols[pl.ds(index, 1), :]
        cell, at_row = cell_and_row(col, cells)
        cell_hot = jnp.where(iota((cells, width), 0) == cell, 1.0, 0.0).astype(BF16)
        product = dot(both, cell_hot)
        product = product[:count] + product[count:]
        row = jnp.broadcast_to(at_row, (levels, width))
        total = jnp.zeros((levels, width), F32)
        for r in range(lat_rows):
            total = jnp.where(row == r, product[r * levels : (r + 1) * levels], total)
        for j in range(per_row):
            out[index * per_row + j] = total[:, j * slots : (j + 1) * slots]
        return carry

    lax.fori_loop(0, cols.shape[0], step, 0, unroll=4)


def to_columns(cols, values, shape):
    levels, lat_rows, cells = shape
    slots = values.shape[2]
    width = cols.shape[1]
    per_row = width // slots
    count = levels * lat_rows

    def step(index, total):
        col = cols[pl.ds(index, 1), :]
        cell, at_row = cell_and_row(col, cells)
        cell_hot = jnp.where(iota((cells, width), 0) == cell, 1.0, 0.0).astype(BF16)
        chosen = iota((lat_rows, width), 0) == at_row
        value = values[index * per_row]
        if per_row > 1:
            value = jnp.concatenate(
                [values[index * per_row + j] for j in range(per_row)], axis=1
            )
        high = value.astype(BF16).astype(F32)
        low = value - high
        parts = [jnp.where(chosen, high[l : l + 1], 0.0) for l in range(levels)]
        parts += [jnp.where(chosen, low[l : l + 1], 0.0) for l in range(levels)]
        return total + dot_nt(jnp.concatenate(parts, axis=0).astype(BF16), cell_hot)

    total = lax.fori_loop(
        0, cols.shape[0], step, jnp.zeros((2 * count, cells), F32), unroll=4
    )
    return (total[:count] + total[count:]).reshape(shape)


def pick(width, group, side, cells):
    row, col = iota((cells, cells), 0), iota((cells, cells), 1)
    member, spot = split(col, width)
    here = row == (spot if side else spot + (cells - width))
    if group is not None:
        here = jnp.logical_and(here, member == group)
    return jnp.where(here, 1.0, 0.0).astype(BF16)


def make_strips(ens, strips):
    _, groups, levels, rows, cells = strips.shape
    each = ens.shape[0] // groups
    width = cells // each
    total = None
    for j in range(each):
        some = jnp.concatenate([ens[g * each + j] for g in range(groups)], axis=0)
        some = some.reshape(groups * levels * rows, cells)
        both = jnp.concatenate([pick(width, j, 0, cells), pick(width, j, 1, cells)], axis=1)
        term = dot(some, both)
        total = term if total is None else total + term
    for side in range(2):
        strips[side] = (
            total[:, side * cells : (side + 1) * cells].astype(BF16).reshape(strips.shape[1:])
        )


def covariance(ens_coef, static_coef, whole, strips, field, lat_op, lon_op, edge_op, edge, out):
    n_lat, members, levels, rows, cells = whole.shape
    groups = strips.shape[2]
    each = members // groups
    some = lat_op.shape[1] // (n_lat * rows)
    parts = each // some
    size = n_lat * some * rows
    width = cells // each
    edge_high, edge_low = edge_op[0], edge_op[1]
    sides = []
    for side in range(2):
        block = field[2 * side * n_lat : (2 * side + 1) * n_lat]
        high, low = halves(block.reshape(n_lat * levels * rows, cells))
        tile = pick(width, None, side, cells)
        sides.append((dot(high, tile) + dot(low, tile)).reshape(n_lat, levels, rows, cells))
    for a in range(n_lat):
        wide = []
        for side in range(2):
            h = sides[side][a]
            terms = (strips[side, a].astype(F32) * h[None]).reshape(groups * levels * rows, cells)
            wide.append(jnp.concatenate([terms, h.reshape(levels * rows, cells)], axis=0))
        high, low = halves(jnp.concatenate(wide, axis=1))
        edge[a] = (
            dot(high, edge_high) + dot(high, edge_low) + dot(low, edge_high)
        ).reshape(edge.shape[1:])
    lon_high, lon_low = lon_op[0], lon_op[1]

    def smooth(pieces, group, width_of):
        lanes = []
        for index, (l, p, piece) in enumerate(pieces):
            lanes.append(piece.reshape(size, cells))
        count = len(lanes)
        if count % 2:
            lanes.append(jnp.zeros((size, cells), F32))
        results = []
        for first in range(0, count, 2):
            high, low = halves(jnp.concatenate(lanes[first : first + 2], axis=1))
            mid = dot(high, lon_high) + dot(high, lon_low) + dot(low, lon_high)
            extra = []
            for l, p, piece in pieces[first : first + 2]:
                at = [width_of(p * some + j) for j in range(some)]
                extra.append(
                    jnp.stack(
                        [edge[:, group, l, :, x * cells : (x + 1) * cells] for x in at], axis=1
                    ).reshape(size, cells)
                )
            if len(extra) == 1:
                extra.append(jnp.zeros((size, cells), F32))
            high, low = halves(mid + jnp.concatenate(extra, axis=1))
            both = dot(lat_op[...], high)
            done = both[:size] + both[size:] + dot(lat_op[:size], low)
            for index in range(min(2, count - first)):
                results.append(
                    done[:, index * cells : (index + 1) * cells].reshape(n_lat, some, rows, cells)
                )
        return results

    own = [field[n_lat : 2 * n_lat, l] for l in range(levels)]

    def step(group, total):
        pieces, kept = [], []
        for l in range(levels):
            for p in range(parts):
                values = whole[:, pl.ds(group * each + p * some, some), l].astype(F32)
                kept.append((l, values))
                pieces.append((l, p, values * own[l][:, None]))
        done = smooth(pieces, group, lambda x: x)
        total = list(total)
        for (l, values), result in zip(kept, done):
            total[l] = total[l] + jnp.sum(values * result, axis=1)
        return tuple(total)

    zero = jnp.zeros((n_lat, rows, cells), F32)
    total = lax.fori_loop(0, groups, step, (zero,) * levels)
    pieces = []
    for l in range(levels):
        piece = [own[l]] + [zero] * (some - 1)
        pieces.append((l, 0, jnp.stack(piece, axis=1)))
    done = smooth(pieces, groups, lambda x: 0)
    for l in range(levels):
        out[:, l] = ens_coef * total[l] + static_coef[l] * done[l][:, 0]


def banded(taps, offset):
    total = jnp.zeros(offset.shape, F32)
    for t in range(len(taps)):
        total = jnp.where(offset == t, taps[t], total)
    return total


def store_halves(ref, value):
    ref[0], ref[1] = halves(value)


def edge_operator(taps, reach, each, cells, op):
    width = cells // each
    row, col = iota((2 * cells, cells), 0), iota((2 * cells, cells), 1)
    side, lane = split(row, cells)
    member, spot = split(lane, width)
    at = jnp.where(side == 0, spot - width, spot + cells)
    value = banded(taps, at - col + reach)
    for j in range(each):
        high, low = halves(jnp.where(member == j, value, 0.0))
        op[0, :, j * cells : (j + 1) * cells] = high
        op[1, :, j * cells : (j + 1) * cells] = low


def pair_operator(taps, reach, cells, op):
    row, col = iota((2 * cells, 2 * cells), 0), iota((2 * cells, 2 * cells), 1)
    row_block, row_at = split(row, cells)
    col_block, col_at = split(col, cells)
    store_halves(
        op, jnp.where(row_block == col_block, banded(taps, row_at - col_at + reach), 0.0)
    )


def make_operators(n_lat, rows, cells, each, lat_taps, lon_taps, lat_op, lon_op, edge_op):
    count = lat_taps.shape[0]
    half = (count - 1) // 2
    lat = [lat_taps[t] for t in range(count)]
    lon = [lon_taps[t] for t in range(count)]
    size = lat_op.shape[1]
    some = size // (n_lat * rows)
    row, col = iota((size, size), 0), iota((size, size), 1)

    def lat_of(ids):
        outer, r = split(ids, rows)
        a, j = split(outer, some)
        return a * rows + r, j

    row_at, row_member = lat_of(row)
    col_at, col_member = lat_of(col)
    high, low = halves(
        jnp.where(row_member == col_member, banded(lat, col_at - row_at + half), 0.0)
    )
    lat_op[:size], lat_op[size:] = halves(
        dot_nt(high, high) + dot_nt(high, low) + dot_nt(low, high)
    )
    corr = []
    for lag in range(-2 * half, 2 * half + 1):
        terms = [lon[t] * lon[t - lag] for t in range(count) if 0 <= t - lag < count]
        corr.append(functools.reduce(lambda a, b: a + b, terms))
    pair_operator(corr, 2 * half, cells, lon_op)
    edge_operator(corr, 2 * half, each, cells, edge_op)


def make_adjoint_operators(rows, cells, each, lat_taps, lon_taps, lat_op, lon_op, edge_op):
    count = lat_taps.shape[0]
    half = (count - 1) // 2
    lat = [lat_taps[t] for t in range(count)][::-1]
    lon = [lon_taps[t] for t in range(count)][::-1]
    shape = (each * rows, 3 * each * rows)
    row_member, row_at = split(iota(shape, 0), rows)
    outer, col_at = split(iota(shape, 1), rows)
    part, col_member = split(outer, each)
    offset = (part - 1) * rows + col_at - row_at + half
    lat_op[: shape[0]], lat_op[shape[0] :] = halves(
        jnp.where(row_member == col_member, banded(lat, offset), 0.0)
    )
    pair_operator(lon, half, cells, lon_op)
    edge_operator(lon, half, each, cells, edge_op)


def main_kernel(
    n_lat, n_lon, iterations,
    sigma, step, lat_taps, lon_taps, ens, send_count, cols, pos, level, weight, innov, prec,
    departure, near, near_sides, near_held, lat_adjoint, lon_adjoint, edge_adjoint,
    count_row, counts, whole, strips, near_strips, pushed, incoming, held, field, part, part_in,
    packed, table, hi, lo, lat_op, lon_op, edge_op, edge,
    ex_send, ex_recv, near_send, near_recv, side_send, side_recv, held_send, held_recv,
):
    lat_at, lon_at = lax.axis_index("lat"), lax.axis_index("lon")
    me = lat_at * n_lon + lon_at
    devices = n_lat * n_lon
    levels, rows, cells = held.shape
    slots = pushed.shape[2]
    members = ens.shape[0]
    task = levels // n_lat
    each = members // strips.shape[1]

    def place(d):
        return (d // n_lon, d % n_lon)

    barrier = pltpu.get_barrier_semaphore()

    def greet(k, carry):
        pl.semaphore_signal(
            barrier, inc=1, device_id=place((me + k) % devices), device_id_type=MESH
        )
        return carry

    lax.fori_loop(1, devices, greet, 0)
    count_row[...] = jnp.zeros_like(count_row)
    count_row[:, :devices] = send_count[...]
    pl.semaphore_wait(barrier, devices - 1)

    def copy_to(source, target, number, device):
        return pltpu.make_async_remote_copy(
            src_ref=source, dst_ref=target, send_sem=ex_send.at[number],
            recv_sem=ex_recv.at[number], device_id=device, device_id_type=MESH,
        )

    def send(source, target, number):
        def one(k, carry):
            d = (me + k) % devices
            copy_to(source(d), target.at[me], number, place(d)).start()
            return carry

        lax.fori_loop(1, devices, one, 0)

    def wait(target, number, count=devices - 1):
        every = target.at[pl.ds(0, count)]
        copy = copy_to(every, every, number, place((me + 1) % devices))
        copy.wait_send()
        copy.wait_recv()

    def of_task(a):
        return pl.ds(a * task, task)

    def lat_peer(k):
        return (lat_at + k) % n_lat

    def lon_peer(turn):
        return (lon_at + turn + n_lon) % n_lon

    send(lambda d: count_row, counts, 0)
    counts[me] = count_row[...]
    for k in range(1, n_lat):
        a = lat_peer(k)
        copy_to(ens.at[:, of_task(a)], whole.at[lat_at], 1, (a, lon_at)).start()
    whole[lat_at] = ens[:, of_task(lat_at)]
    make_strips(ens, strips)
    for k in range(n_lat):
        a = lat_peer(k)
        for side, turn in enumerate((1, -1)):
            copy_to(
                strips.at[side, :, of_task(a)], near_strips.at[side * n_lat + lat_at], 2,
                (a, lon_peer(turn)),
            ).start()
    wait(counts, 0)
    received = jnp.concatenate([counts[d] for d in range(devices)], axis=0)
    width = received.shape[1]
    column = jnp.sum(
        jnp.where(iota((devices, width), 1) == me, received, 0), axis=1, keepdims=True
    )
    as_row = jnp.sum(
        jnp.where(iota((devices, width), 0) == iota((devices, width), 1), column, 0),
        axis=0, keepdims=True,
    )
    ends = jnp.sum(
        jnp.where(iota((devices, width), 1) <= iota((devices, width), 0), as_row, 0),
        axis=1, keepdims=True,
    )
    for q in range(pos.shape[0]):
        place_q = pos[q : q + 1, :]
        past = place_q >= ends
        source = jnp.sum(jnp.where(past, 1, 0), axis=0, keepdims=True)
        lo[q : q + 1, :] = place_q - jnp.sum(jnp.where(past, column, 0), axis=0, keepdims=True)
        hi[q : q + 1, :] = source * levels + level[...]

    def near_chunk(chunk, begin):
        size = members // CHUNKS
        some = pl.ds(chunk * size, size)
        for index, turn in enumerate((1, -1)):
            exchange_pair(
                begin, *lat_has(n_lat, lat_at, turn),
                src_ref=ens.at[some], dst_ref=near.at[index, some],
                send_sem=near_send.at[index * CHUNKS + chunk],
                recv_sem=near_recv.at[index * CHUNKS + chunk],
                device_id=((lat_at + turn + n_lat) % n_lat, lon_at),
            )

    def side_copies(begin):
        for up, climb in enumerate((1, 0, -1)):
            for side, turn in enumerate((1, -1)):
                exchange_pair(
                    begin, *lat_has(n_lat, lat_at, climb),
                    src_ref=strips.at[side],
                    dst_ref=near_sides.at[up, side],
                    send_sem=side_send.at[up * 2 + side], recv_sem=side_recv.at[up * 2 + side],
                    device_id=((lat_at + climb + n_lat) % n_lat, lon_peer(turn)),
                )

    number = 3
    for iteration in range(iterations):
        before = iteration - 1
        if iteration > 0:
            around = field.at[before]
            for k in range(n_lat):
                a = lat_peer(k)
                for at, turn in enumerate((1, 0, -1)):
                    if k == 0 and turn == 0:
                        continue
                    copy_to(
                        held.at[of_task(a)], around.at[at * n_lat + lat_at], number,
                        (a, lon_peer(turn)),
                    ).start()
            field[before, n_lat + lat_at] = held[of_task(lat_at)]
            if iteration == 1:
                wait(whole, 1, n_lat - 1)
                wait(near_strips, 2, 2 * n_lat)
            wait(around, number, 3 * n_lat - 1)
            if iteration == 1:
                near_chunk(0, True)
                side_copies(True)
            covariance(
                HYBRID_ENSEMBLE**2 / (members - 1),
                [HYBRID_STATIC**2 * sigma[lat_at * task + l] ** 2 for l in range(task)],
                whole, near_strips.reshape(2, n_lat, *near_strips.shape[1:]), around,
                lat_op, lon_op, edge_op, edge, part,
            )
            home = part_in.at[before]
            for k in range(1, n_lat):
                a = lat_peer(k)
                copy_to(part.at[a], home.at[lat_at], number + 1, (a, lon_at)).start()
            part_in[before, lat_at] = part[lat_at]
            wait(home, number + 1, n_lat - 1)
            if iteration == 1:
                near_chunk(1, True)
            to_slots(cols, part_in[before].reshape(levels, rows, cells), packed)
            send(lambda d: packed.at[d], table.at[before], number + 2)
            table[before, me] = packed[me]
            if iteration == 1:
                make_adjoint_operators(
                    rows, cells, each, lat_taps, lon_taps, lat_adjoint, lon_adjoint, edge_adjoint
                )
            wait(table.at[before], number + 2)
            number += 3
            if iteration == 1:
                near_chunk(2, True)
                near_chunk(3, True)
        obs_step(
            table.at[before] if iteration > 0 else None,
            hi, lo, weight, innov, prec, departure, pushed, devices * levels, slots,
        )
        send(lambda d: pushed.at[d], incoming.at[iteration], number)
        incoming[iteration, me] = pushed[me]
        if iteration == 0:
            make_operators(
                n_lat, rows, cells, each, lat_taps, lon_taps, lat_op, lon_op, edge_op
            )
        wait(incoming.at[iteration], number)
        number += 1
        forcing = to_columns(cols, incoming.at[iteration], held.shape)
        if iteration == 0:
            held[...] = -step[0] * forcing
        else:
            held[...] = held[...] - step[iteration] * (forcing + held[...])

    held_copies(n_lat, n_lon, lat_at, lon_at, held, near_held, held_send, held_recv, True)
    near_held[1, 1] = held[...]
    for chunk in range(CHUNKS):
        near_chunk(chunk, False)
    side_copies(False)
    held_copies(n_lat, n_lon, lat_at, lon_at, held, near_held, held_send, held_recv, False)


def exchange_pair(begin, has_send, has_recv, **copy):
    made = pltpu.make_async_remote_copy(device_id_type=MESH, **copy)
    if begin:
        pl.when(has_send)(made.start)
    else:
        pl.when(has_send)(made.wait_send)
        pl.when(has_recv)(made.wait_recv)


def lat_has(n_lat, lat_at, step):
    send = jnp.logical_and(lat_at + step >= 0, lat_at + step < n_lat)
    recv = jnp.logical_and(lat_at - step >= 0, lat_at - step < n_lat)
    return send, recv


def held_copies(n_lat, n_lon, lat_at, lon_at, held, near_held, held_send, held_recv, begin):
    for up, step in enumerate((1, 0, -1)):
        has = lat_has(n_lat, lat_at, step)
        for side, turn in enumerate((1, 0, -1)):
            if step == 0 and turn == 0:
                continue
            exchange_pair(
                begin, *has,
                src_ref=held, dst_ref=near_held.at[up, side],
                send_sem=held_send.at[up * 3 + side], recv_sem=held_recv.at[up * 3 + side],
                device_id=((lat_at + step + n_lat) % n_lat, (lon_at + turn + n_lon) % n_lon),
            )


def adjoint_kernel(
    scale, n_lat,
    sigma, members, near, sides, field, lon_op, lat_op, edge_op, departure,
    out, static_out, departure_out,
    own, edge_field, edge,
):
    batch, levels, rows, cells = out.shape
    groups = sides.shape[2]
    each = edge_op.shape[2] // cells
    width = cells // each
    lat_at = lax.axis_index("lat")
    keep = (lat_at > 0, None, lat_at < n_lat - 1)
    lon_high, lon_low = lon_op[0], lon_op[1]
    size = lat_op.shape[0] // 2

    def kept(part, value):
        return value if keep[part] is None else jnp.where(keep[part], value, 0.0)

    def along_lat(stacked):
        high, low = halves(stacked)
        both = dot(lat_op[...], high)
        return both[:size] + both[size:] + dot(lat_op[:size], low)

    def along_lon(stacked):
        high, low = halves(stacked)
        return dot(high, lon_high) + dot(high, lon_low) + dot(low, lon_high)

    @pl.when(pl.program_id(0) == 0)
    def _():
        departure_out[...] = departure[...]
        for part in range(3):
            own[part] = kept(part, field[part, 1])
            for side in range(2):
                value = kept(part, field[part, 2 * side]).reshape(levels * rows, cells)
                high, low = halves(value)
                tile = pick(width, None, side, cells)
                edge_field[part, side] = (dot(high, tile) + dot(low, tile)).reshape(
                    levels, rows, cells
                )

        def edge_of(group):
            results = []
            for first in range(0, levels, each):
                pieces = []
                for part in range(3):
                    lanes = []
                    for side in range(2):
                        value = edge_field[part, side, first : first + each]
                        if group is not None:
                            some = sides[part, side, group, first : first + each].astype(F32)
                            value = kept(part, some * value)
                        lanes.append(value.reshape(size, cells))
                    pieces.append(jnp.concatenate(lanes, axis=1))
                results.append(along_lat(jnp.concatenate(pieces, axis=0)))
            return results

        stacked = jnp.concatenate(
            [piece for g in list(range(groups)) + [None] for piece in edge_of(g)], axis=0
        )
        high, low = halves(stacked)
        edge[...] = (
            dot(high, edge_op[0]) + dot(high, edge_op[1]) + dot(low, edge_op[0])
        ).reshape(edge.shape)
        results = []
        for first in range(0, levels, each):
            stacked = jnp.concatenate(
                [own[part, first : first + each].reshape(size, cells) for part in range(3)], axis=0
            )
            both = jnp.concatenate([stacked, jnp.zeros_like(stacked)], axis=1)
            results.append(along_lat(both))
        smooth = along_lon(jnp.concatenate(results, axis=0))[:, :cells].reshape(
            levels, rows, cells
        )
        for l in range(levels):
            static_out[l] = (HYBRID_STATIC * sigma[l]) * (
                smooth[l] + edge[groups, l, :, :cells]
            )

    for g in range(batch // each):
        some = pl.ds(g * each, each)
        group = pl.program_id(0) * (batch // each) + g
        results = []
        for first in range(0, levels, 2):
            pieces = []
            for part in range(3):
                lanes = []
                for l in range(first, min(first + 2, levels)):
                    values = members[some, l] if part == 1 else near[part // 2, some, l]
                    lanes.append(
                        kept(part, values.astype(F32) * own[part, l][None]).reshape(size, cells)
                    )
                if len(lanes) == 1:
                    lanes.append(jnp.zeros((size, cells), F32))
                pieces.append(jnp.concatenate(lanes, axis=1))
            results.append(along_lat(jnp.concatenate(pieces, axis=0)))
        smooth = along_lon(jnp.concatenate(results, axis=0))
        for l in range(levels):
            block = smooth[l // 2 * size : (l // 2 + 1) * size]
            block = block[:, l % 2 * cells : (l % 2 + 1) * cells].reshape(each, rows, cells)
            extra = jnp.stack(
                [edge[group, l, :, j * cells : (j + 1) * cells] for j in range(each)], axis=0
            )
            out[some, l] = scale * (block + extra)


def divisor(count, limit):
    return max(n for n in range(1, count + 1) if count % n == 0 and (n <= limit or n == 1))


def per_device(
    ensemble,
    static_sigma,
    lat_taps,
    lon_taps,
    step_len,
    send_cols,
    send_count,
    obs_ref,
    obs_level,
    obs_weight,
    innovation,
    obs_precision,
):
    members, levels, rows, cells = ensemble.shape
    half = (lat_taps.shape[0] - 1) // 2
    n_lat, n_lon = lax.axis_size("lat"), lax.axis_size("lon")
    devices = n_lat * n_lon
    slots = send_cols.shape[3]
    scale = HYBRID_ENSEMBLE / math.sqrt(members - 1)

    positions = obs_ref.reshape(obs_ref.shape[2], -1)
    weight = obs_weight.reshape(positions.shape)
    task = levels // n_lat
    each = cells // (2 * half)
    groups = members // each
    assert task * n_lat == levels and each * 2 * half == cells and groups * each == members
    assert levels % each == 0

    wide_slots = max(slots, 256)
    cols = send_cols.reshape(-1, wide_slots)
    iterations = step_len.shape[0]
    some = divisor(each, max(1, 256 // (n_lat * rows)))
    lat_size = n_lat * rows * some
    later = max(1, iterations - 1)
    count_width = -(-devices // 128) * 128
    smem = pl.BlockSpec(memory_space=pltpu.SMEM)
    hbm = pl.BlockSpec(memory_space=pl.ANY)
    exchanges = 3 + iterations + 3 * (iterations - 1)
    strip = (groups, levels, rows, cells)
    lat_shape = (2 * each * rows, 3 * each * rows)
    pair_shape = (2, 2 * cells, 2 * cells)
    edge_shape = (2, 2 * cells, each * cells)
    departure, near, near_sides, near_held, lat_adjoint, lon_adjoint, edge_adjoint = pl.pallas_call(
        functools.partial(main_kernel, n_lat, n_lon, iterations),
        out_shape=(
            jax.ShapeDtypeStruct((1, positions.shape[1]), F32),
            jax.ShapeDtypeStruct((2,) + ensemble.shape, BF16),
            jax.ShapeDtypeStruct((3, 2) + strip, BF16),
            jax.ShapeDtypeStruct((3, 3, levels, rows, cells), F32),
            jax.ShapeDtypeStruct(lat_shape, BF16),
            jax.ShapeDtypeStruct(pair_shape, BF16),
            jax.ShapeDtypeStruct(edge_shape, BF16),
        ),
        in_specs=[smem] * 4 + [VMEM] * 8,
        out_specs=(VMEM, hbm, VMEM, VMEM, VMEM, VMEM, VMEM),
        scratch_shapes=[
            pltpu.VMEM((1, count_width), jnp.int32),
            pltpu.VMEM((devices, 1, count_width), jnp.int32),
            pltpu.VMEM((n_lat, members, task, rows, cells), BF16),
            pltpu.VMEM((2,) + strip, BF16),
            pltpu.VMEM((2 * n_lat, groups, task, rows, cells), BF16),
            pltpu.VMEM((devices, levels, slots), F32),
            pltpu.VMEM((iterations, devices, levels, slots), F32),
            pltpu.VMEM((levels, rows, cells), F32),
            pltpu.VMEM((later, 3 * n_lat, task, rows, cells), F32),
            pltpu.VMEM((n_lat, task, rows, cells), F32),
            pltpu.VMEM((later, n_lat, task, rows, cells), F32),
            pltpu.VMEM((devices, levels, slots), F32),
            pltpu.VMEM((later, devices, levels, slots), F32),
            pltpu.VMEM(positions.shape, jnp.int32),
            pltpu.VMEM(positions.shape, jnp.int32),
            pltpu.VMEM((2 * lat_size, lat_size), BF16),
            pltpu.VMEM(pair_shape, BF16),
            pltpu.VMEM(edge_shape, BF16),
            pltpu.VMEM((n_lat, groups + 1, task, rows, each * cells), F32),
            pltpu.SemaphoreType.DMA((exchanges,)),
            pltpu.SemaphoreType.DMA((exchanges,)),
            pltpu.SemaphoreType.DMA((2 * CHUNKS,)),
            pltpu.SemaphoreType.DMA((2 * CHUNKS,)),
            pltpu.SemaphoreType.DMA((6,)),
            pltpu.SemaphoreType.DMA((6,)),
            pltpu.SemaphoreType.DMA((9,)),
            pltpu.SemaphoreType.DMA((9,)),
        ],
        compiler_params=pltpu.CompilerParams(
            collective_id=0, has_side_effects=True, vmem_limit_bytes=VMEM_LIMIT
        ),
        name="analysis",
    )(
        static_sigma, step_len, lat_taps, lon_taps, ensemble, send_count.reshape(1, -1), cols,
        positions, obs_level.reshape(1, -1), weight, innovation.reshape(1, -1),
        obs_precision.reshape(1, -1),
    )
    batch = each * divisor(groups, 1)
    own_spec = pl.BlockSpec((batch, levels, rows, cells), lambda k: (k, 0, 0, 0))
    near_spec = pl.BlockSpec((2, batch, levels, rows, cells), lambda k: (0, k, 0, 0, 0))
    control, static, departure = pl.pallas_call(
        functools.partial(adjoint_kernel, scale, n_lat),
        grid=(members // batch,),
        out_shape=(
            jax.ShapeDtypeStruct(ensemble.shape, F32),
            jax.ShapeDtypeStruct((levels, rows, cells), F32),
            jax.ShapeDtypeStruct(departure.shape, F32),
        ),
        in_specs=[smem, own_spec, near_spec] + [VMEM] * 6,
        out_specs=(
            pl.BlockSpec((batch, levels, rows, cells), lambda k: (k, 0, 0, 0)),
            pl.BlockSpec((levels, rows, cells), lambda k: (0, 0, 0)),
            pl.BlockSpec(departure.shape, lambda k: (0, 0)),
        ),
        scratch_shapes=[
            pltpu.VMEM((3, levels, rows, cells), F32),
            pltpu.VMEM((3, 2, levels, rows, cells), F32),
            pltpu.VMEM((groups + 1, levels, rows, each * cells), F32),
        ],
        compiler_params=pltpu.CompilerParams(vmem_limit_bytes=VMEM_LIMIT),
        name="adjoint",
    )(
        static_sigma, ensemble, near, near_sides, near_held, lon_adjoint, lat_adjoint,
        edge_adjoint, departure,
    )
    return control, static, departure.reshape(1, 1, -1)


def solution(mesh):
    return jax.shard_map(
        per_device,
        mesh=mesh,
        in_specs=(
            P(None, None, "lat", "lon"),
            P(),
            P(),
            P(),
            P(),
            P("lat", "lon", None, None),
            P("lat", "lon", None),
            P("lat", "lon", None, None),
            P("lat", "lon", None),
            P("lat", "lon", None, None),
            P("lat", "lon", None),
            P("lat", "lon", None),
        ),
        out_specs=(P(None, None, "lat", "lon"), P(None, "lat", "lon"), P("lat", "lon", None)),
        check_vma=False,
    )
```

```python
import functools
import math

import jax
import jax.numpy as jnp
from jax import lax
from jax.experimental import pallas as pl
from jax.experimental.pallas import tpu as pltpu
from jax.sharding import PartitionSpec as P

HYBRID_STATIC = 0.5
HYBRID_ENSEMBLE = 0.8660254037844386
BF16 = jnp.bfloat16
F32 = jnp.float32
MESH = pl.DeviceIdType.MESH
CHUNKS = 4
LANES = 128
STEPS = 16383.0
VMEM_LIMIT = 60 * 2**20
VMEM = pl.BlockSpec(memory_space=pltpu.VMEM)


def halves(x):
    high = x.astype(BF16)
    return high, (x - high.astype(F32)).astype(BF16)


def dot(a, b):
    return jnp.dot(a, b, preferred_element_type=F32)


def dot_nt(a, b):
    return lax.dot_general(a, b, (((1,), (1,)), ((), ())), preferred_element_type=F32)


def dot3(a, b):
    a_high, a_low = halves(a)
    b_high, b_low = halves(b)
    return dot(a_high, b_high) + dot(a_high, b_low) + dot(a_low, b_high)


def iota(shape, dim):
    return lax.broadcasted_iota(jnp.int32, shape, dim)


def obs_step(table, hi, lo, weight, innov, prec, departure, out, rows, slots):
    chunk = 1024 if rows <= 256 else 256
    points = hi.shape[0]
    if table is not None:
        table_both = jnp.concatenate(halves(table[...].reshape(rows, slots)), axis=0)

    def step(index, carry):
        where = pl.ds(pl.multiple_of(index * chunk, chunk), chunk)
        row_ids = iota((rows, chunk), 0)
        slot_ids = iota((slots, chunk), 0)
        value = -innov[:, where]
        if table is not None:
            for q in range(points):
                lo_hot = jnp.where(slot_ids == lo[q : q + 1, where], 1.0, 0.0).astype(BF16)
                product = dot(table_both, lo_hot)
                product = product[:rows] + product[rows:]
                picked = jnp.sum(
                    jnp.where(row_ids == hi[q : q + 1, where], product, 0.0), axis=0, keepdims=True
                )
                value = value + weight[q : q + 1, where] * picked
            departure[:, where] = value
        value = prec[:, where] * value
        total = None
        for q in range(points):
            lo_hot = jnp.where(slot_ids == lo[q : q + 1, where], 1.0, 0.0).astype(BF16)
            pushed = weight[q : q + 1, where] * value
            high = pushed.astype(BF16).astype(F32)
            chosen = row_ids == hi[q : q + 1, where]
            both = jnp.concatenate(
                [jnp.where(chosen, high, 0.0), jnp.where(chosen, pushed - high, 0.0)], axis=0
            ).astype(BF16)
            term = dot_nt(both, lo_hot)
            term = term[:rows] + term[rows:]
            total = term if total is None else total + term
        return carry + total

    total = lax.fori_loop(0, hi.shape[1] // chunk, step, jnp.zeros((rows, slots), F32))
    out[...] = total.reshape(out.shape)


def encode(values, out):
    devices, levels, slots = values.shape
    lane = iota((devices, levels, LANES), 2)
    codes = []
    for first in range(0, slots, LANES):
        value = values[:, :, first : first + LANES]
        top = jnp.max(jnp.abs(value), axis=2, keepdims=True)
        power = jnp.clip(jnp.ceil(jnp.log2(jnp.maximum(top, 1e-30))), -99.0, 120.0)
        value = jnp.clip(jnp.floor(value * (STEPS * jnp.exp2(-power)) + 0.5), -STEPS, STEPS)
        shift = jnp.broadcast_to(power.astype(jnp.int32) + 128, lane.shape)
        bit = jnp.bitwise_and(jnp.right_shift(shift, jnp.bitwise_and(lane, 7)), 1)
        codes.append(2 * value.astype(jnp.int32) + bit)
    out[...] = jnp.concatenate(codes, axis=1).astype(jnp.int16)


def decode(coded, out):
    devices, levels, slots = out.shape
    code = coded[...].astype(jnp.int32)
    for piece in range(slots // LANES):
        some = code[:, piece * levels : (piece + 1) * levels]
        bit = jnp.bitwise_and(some, 1).astype(F32).reshape(devices * levels, LANES)
        row = iota((LANES, LANES), 0)
        worth = jnp.where(row < 8, jnp.exp2(row.astype(F32)), 0.0).astype(BF16)
        power = dot(bit.astype(BF16), worth).reshape(some.shape) - 128.0
        value = jnp.right_shift(some, 1).astype(F32) * (jnp.exp2(power) * (1.0 / STEPS))
        out[:, :, piece * LANES : (piece + 1) * LANES] = value


def cell_and_row(col, cells):
    if cells & (cells - 1):
        return col % cells, col // cells
    return jnp.bitwise_and(col, cells - 1), jnp.right_shift(col, cells.bit_length() - 1)


def split(ids, size):
    inner, outer = cell_and_row(ids, size)
    return outer, inner


def to_slots(cols, field, out):
    levels, lat_rows, cells = field.shape
    slots = out.shape[2]
    width = cols.shape[1]
    per_row = width // slots
    rows = jnp.concatenate([field[:, r, :] for r in range(lat_rows)], axis=0)
    count = rows.shape[0]
    both = jnp.concatenate(halves(rows), axis=0)

    def step(index, carry):
        col = cols[pl.ds(index, 1), :]
        cell, at_row = cell_and_row(col, cells)
        cell_hot = jnp.where(iota((cells, width), 0) == cell, 1.0, 0.0).astype(BF16)
        product = dot(both, cell_hot)
        product = product[:count] + product[count:]
        row = jnp.broadcast_to(at_row, (levels, width))
        total = jnp.zeros((levels, width), F32)
        for r in range(lat_rows):
            total = jnp.where(row == r, product[r * levels : (r + 1) * levels], total)
        for j in range(per_row):
            out[index * per_row + j] = total[:, j * slots : (j + 1) * slots]
        return carry

    lax.fori_loop(0, cols.shape[0], step, 0, unroll=4)


def to_columns(cols, values, shape):
    levels, lat_rows, cells = shape
    slots = values.shape[2]
    width = cols.shape[1]
    per_row = width // slots
    count = levels * lat_rows

    def step(index, total):
        col = cols[pl.ds(index, 1), :]
        cell, at_row = cell_and_row(col, cells)
        cell_hot = jnp.where(iota((cells, width), 0) == cell, 1.0, 0.0).astype(BF16)
        chosen = iota((lat_rows, width), 0) == at_row
        value = values[index * per_row]
        if per_row > 1:
            value = jnp.concatenate(
                [values[index * per_row + j] for j in range(per_row)], axis=1
            )
        high = value.astype(BF16).astype(F32)
        low = value - high
        parts = [jnp.where(chosen, high[l : l + 1], 0.0) for l in range(levels)]
        parts += [jnp.where(chosen, low[l : l + 1], 0.0) for l in range(levels)]
        return total + dot_nt(jnp.concatenate(parts, axis=0).astype(BF16), cell_hot)

    total = lax.fori_loop(
        0, cols.shape[0], step, jnp.zeros((2 * count, cells), F32), unroll=4
    )
    return (total[:count] + total[count:]).reshape(shape)


def pick(width, group, side, cells):
    row, col = iota((cells, cells), 0), iota((cells, cells), 1)
    member, spot = split(col, width)
    here = row == (spot if side else spot + (cells - width))
    if group is not None:
        here = jnp.logical_and(here, member == group)
    return jnp.where(here, 1.0, 0.0).astype(BF16)


def make_strips(ens, strips):
    _, groups, levels, rows, cells = strips.shape
    each = ens.shape[0] // groups
    width = cells // each
    total = None
    for j in range(each):
        some = jnp.concatenate([ens[g * each + j] for g in range(groups)], axis=0)
        some = some.reshape(groups * levels * rows, cells)
        both = jnp.concatenate([pick(width, j, 0, cells), pick(width, j, 1, cells)], axis=1)
        term = dot(some, both)
        total = term if total is None else total + term
    for side in range(2):
        strips[side] = (
            total[:, side * cells : (side + 1) * cells].astype(BF16).reshape(strips.shape[1:])
        )


def covariance(ens_coef, static_coef, whole, strips, field, lat_op, lon_op, edge_op, edge, out):
    n_lat, members, levels, rows, cells = whole.shape
    groups = strips.shape[2]
    each = members // groups
    some = lat_op.shape[1] // (n_lat * rows)
    parts = each // some
    size = n_lat * some * rows
    width = cells // each
    edge_high, edge_low = edge_op[0], edge_op[1]
    sides = []
    for side in range(2):
        block = field[2 * side * n_lat : (2 * side + 1) * n_lat]
        high, low = halves(block.reshape(n_lat * levels * rows, cells))
        tile = pick(width, None, side, cells)
        sides.append((dot(high, tile) + dot(low, tile)).reshape(n_lat, levels, rows, cells))
    for a in range(n_lat):
        wide = []
        for side in range(2):
            h = sides[side][a]
            terms = (strips[side, a].astype(F32) * h[None]).reshape(groups * levels * rows, cells)
            wide.append(jnp.concatenate([terms, h.reshape(levels * rows, cells)], axis=0))
        high, low = halves(jnp.concatenate(wide, axis=1))
        edge[a] = (
            dot(high, edge_high) + dot(high, edge_low) + dot(low, edge_high)
        ).reshape(edge.shape[1:])
    lon_high, lon_low = lon_op[0], lon_op[1]

    def smooth(pieces, group, width_of):
        lanes = []
        for index, (l, p, piece) in enumerate(pieces):
            lanes.append(piece.reshape(size, cells))
        count = len(lanes)
        if count % 2:
            lanes.append(jnp.zeros((size, cells), F32))
        results = []
        for first in range(0, count, 2):
            high, low = halves(jnp.concatenate(lanes[first : first + 2], axis=1))
            mid = dot(high, lon_high) + dot(high, lon_low) + dot(low, lon_high)
            extra = []
            for l, p, piece in pieces[first : first + 2]:
                at = [width_of(p * some + j) for j in range(some)]
                extra.append(
                    jnp.stack(
                        [edge[:, group, l, :, x * cells : (x + 1) * cells] for x in at], axis=1
                    ).reshape(size, cells)
                )
            if len(extra) == 1:
                extra.append(jnp.zeros((size, cells), F32))
            high, low = halves(mid + jnp.concatenate(extra, axis=1))
            both = dot(lat_op[...], high)
            done = both[:size] + both[size:] + dot(lat_op[:size], low)
            for index in range(min(2, count - first)):
                results.append(
                    done[:, index * cells : (index + 1) * cells].reshape(n_lat, some, rows, cells)
                )
        return results

    own = [field[n_lat : 2 * n_lat, l] for l in range(levels)]

    def step(group, total):
        pieces, kept = [], []
        for l in range(levels):
            for p in range(parts):
                values = whole[:, pl.ds(group * each + p * some, some), l].astype(F32)
                kept.append((l, values))
                pieces.append((l, p, values * own[l][:, None]))
        done = smooth(pieces, group, lambda x: x)
        total = list(total)
        for (l, values), result in zip(kept, done):
            total[l] = total[l] + jnp.sum(values * result, axis=1)
        return tuple(total)

    zero = jnp.zeros((n_lat, rows, cells), F32)
    total = lax.fori_loop(0, groups, step, (zero,) * levels)
    pieces = []
    for l in range(levels):
        piece = [own[l]] + [zero] * (some - 1)
        pieces.append((l, 0, jnp.stack(piece, axis=1)))
    done = smooth(pieces, groups, lambda x: 0)
    for l in range(levels):
        out[:, l] = ens_coef * total[l] + static_coef[l] * done[l][:, 0]


def banded(taps, offset):
    total = jnp.zeros(offset.shape, F32)
    for t in range(len(taps)):
        total = jnp.where(offset == t, taps[t], total)
    return total


def store_halves(ref, value):
    ref[0], ref[1] = halves(value)


def edge_operator(taps, reach, each, cells, op):
    width = cells // each
    row, col = iota((2 * cells, cells), 0), iota((2 * cells, cells), 1)
    side, lane = split(row, cells)
    member, spot = split(lane, width)
    at = jnp.where(side == 0, spot - width, spot + cells)
    value = banded(taps, at - col + reach)
    for j in range(each):
        high, low = halves(jnp.where(member == j, value, 0.0))
        op[0, :, j * cells : (j + 1) * cells] = high
        op[1, :, j * cells : (j + 1) * cells] = low


def pair_operator(taps, reach, cells, op):
    row, col = iota((2 * cells, 2 * cells), 0), iota((2 * cells, 2 * cells), 1)
    row_block, row_at = split(row, cells)
    col_block, col_at = split(col, cells)
    store_halves(
        op, jnp.where(row_block == col_block, banded(taps, row_at - col_at + reach), 0.0)
    )


def make_operators(n_lat, rows, cells, each, lat_taps, lon_taps, lat_op, lon_op, edge_op):
    count = lat_taps.shape[0]
    half = (count - 1) // 2
    lat = [lat_taps[t] for t in range(count)]
    lon = [lon_taps[t] for t in range(count)]
    size = lat_op.shape[1]
    some = size // (n_lat * rows)
    row, col = iota((size, size), 0), iota((size, size), 1)

    def lat_of(ids):
        outer, r = split(ids, rows)
        a, j = split(outer, some)
        return a * rows + r, j

    row_at, row_member = lat_of(row)
    col_at, col_member = lat_of(col)
    high, low = halves(
        jnp.where(row_member == col_member, banded(lat, col_at - row_at + half), 0.0)
    )
    lat_op[:size], lat_op[size:] = halves(
        dot_nt(high, high) + dot_nt(high, low) + dot_nt(low, high)
    )
    corr = []
    for lag in range(-2 * half, 2 * half + 1):
        terms = [lon[t] * lon[t - lag] for t in range(count) if 0 <= t - lag < count]
        corr.append(functools.reduce(lambda a, b: a + b, terms))
    pair_operator(corr, 2 * half, cells, lon_op)
    edge_operator(corr, 2 * half, each, cells, edge_op)


def make_adjoint_operators(rows, each, packed, cells, lat_taps, lon_taps, lat_op, lon_op, edge_op):
    count = lat_taps.shape[0]
    half = (count - 1) // 2
    lat = [lat_taps[t] for t in range(count)][::-1]
    lon = [lon_taps[t] for t in range(count)][::-1]
    shape = (each * rows, 3 * each * rows)
    row_member, row_at = split(iota(shape, 0), rows)
    outer, col_at = split(iota(shape, 1), rows)
    part, col_member = split(outer, each)
    offset = (part - 1) * rows + col_at - row_at + half
    lat_op[: shape[0]], lat_op[shape[0] :] = halves(
        jnp.where(row_member == col_member, banded(lat, offset), 0.0)
    )
    pair_operator(lon, half, cells, lon_op)
    edge_operator(lon, half, packed, cells, edge_op)


def main_kernel(n_lat, n_lon, iterations, narrow, *refs):
    if not narrow:
        at = 33
        refs = refs[:at] + (None, None) + refs[at:]
    main_body(n_lat, n_lon, iterations, *refs)


def main_body(
    n_lat, n_lon, iterations,
    sigma, step, lat_taps, lon_taps, ens_far, count_far, cols_far, pos_far, level_far, weight_far,
    innov_far, prec_far,
    departure, near, near_sides, near_held, lat_adjoint, lon_adjoint, edge_adjoint,
    count_row, counts, whole, strips, side_strips, near_strips, pushed, incoming, held, field, part, part_in,
    packed, table, coded, arrived, hi, lo, lat_op, lon_op, edge_op, edge,
    ens, send_count, cols, pos, level, weight, innov, prec,
    ex_send, ex_recv, near_send, near_recv, side_send, side_recv, held_send, held_recv, load_sem,
):
    lat_at, lon_at = lax.axis_index("lat"), lax.axis_index("lon")
    me = lat_at * n_lon + lon_at
    devices = n_lat * n_lon
    levels, rows, cells = held.shape
    slots = pushed.shape[2]
    members = ens.shape[0]
    task = levels // n_lat
    each = members // strips.shape[1]

    def place(d):
        return (d // n_lon, d % n_lon)

    barrier = pltpu.get_barrier_semaphore()

    def greet(k, carry):
        pl.semaphore_signal(
            barrier, inc=1, device_id=place((me + k) % devices), device_id_type=MESH
        )
        return carry

    lax.fori_loop(1, devices, greet, 0)
    loads = [
        pltpu.make_async_copy(far, here, load_sem.at[index])
        for index, (far, here) in enumerate(
            (
                (count_far, send_count), (ens_far, ens), (pos_far, pos), (level_far, level),
                (weight_far, weight), (innov_far, innov), (prec_far, prec), (cols_far, cols),
            )
        )
    ]
    for load in loads:
        load.start()
    count_row[...] = jnp.zeros_like(count_row)
    loads[0].wait()
    count_row[:, :devices] = send_count[...]
    pl.semaphore_wait(barrier, devices - 1)

    def copy_to(source, target, number, device):
        return pltpu.make_async_remote_copy(
            src_ref=source, dst_ref=target, send_sem=ex_send.at[number],
            recv_sem=ex_recv.at[number], device_id=device, device_id_type=MESH,
        )

    def send(source, target, number):
        def one(k, carry):
            d = (me + k) % devices
            copy_to(source(d), target.at[me], number, place(d)).start()
            return carry

        lax.fori_loop(1, devices, one, 0)

    def wait(target, number, count=devices - 1):
        every = target.at[pl.ds(0, count)]
        copy = copy_to(every, every, number, place((me + 1) % devices))
        copy.wait_send()
        copy.wait_recv()

    def exchange(values, target, number, meanwhile=None):
        if coded is None:
            send(lambda d: values.at[d], target, number)
            target[me] = values[me]
        else:
            index = number - 3
            encode(values, coded)
            send(lambda d: coded.at[d], arrived.at[index], number)
            arrived[index, me] = coded[me]
        if meanwhile is not None:
            meanwhile()
        if coded is None:
            wait(target, number)
        else:
            wait(arrived.at[index], number)
            decode(arrived.at[index], target)

    def of_task(a):
        return pl.ds(a * task, task)

    def lat_peer(k):
        return (lat_at + k) % n_lat

    def lon_peer(turn):
        return (lon_at + turn + n_lon) % n_lon

    send(lambda d: count_row, counts, 0)
    counts[me] = count_row[...]
    for k in range(1, n_lat):
        a = lat_peer(k)
        copy_to(ens_far.at[:, of_task(a)], whole.at[lat_at], 1, (a, lon_at)).start()
    loads[1].wait()
    whole[lat_at] = ens[:, of_task(lat_at)]
    make_strips(ens, strips)
    for k in range(n_lat):
        a = lat_peer(k)
        for side, turn in enumerate((1, -1)):
            copy_to(
                strips.at[side, :, of_task(a)], near_strips.at[side * n_lat + lat_at], 2,
                (a, lon_peer(turn)),
            ).start()
    for load in loads[2:]:
        load.wait()
    wait(counts, 0)
    received = jnp.concatenate([counts[d] for d in range(devices)], axis=0)
    width = received.shape[1]
    column = jnp.sum(
        jnp.where(iota((devices, width), 1) == me, received, 0), axis=1, keepdims=True
    )
    as_row = jnp.sum(
        jnp.where(iota((devices, width), 0) == iota((devices, width), 1), column, 0),
        axis=0, keepdims=True,
    )
    ends = jnp.sum(
        jnp.where(iota((devices, width), 1) <= iota((devices, width), 0), as_row, 0),
        axis=1, keepdims=True,
    )
    for q in range(pos.shape[0]):
        place_q = pos[q : q + 1, :]
        past = place_q >= ends
        source = jnp.sum(jnp.where(past, 1, 0), axis=0, keepdims=True)
        lo[q : q + 1, :] = place_q - jnp.sum(jnp.where(past, column, 0), axis=0, keepdims=True)
        hi[q : q + 1, :] = source * levels + level[...]

    def near_chunk(chunk, begin):
        size = members // CHUNKS
        some = pl.ds(chunk * size, size)
        for index, turn in enumerate((1, -1)):
            exchange_pair(
                begin, *lat_has(n_lat, lat_at, turn),
                src_ref=ens_far.at[some], dst_ref=near.at[index, some],
                send_sem=near_send.at[index * CHUNKS + chunk],
                recv_sem=near_recv.at[index * CHUNKS + chunk],
                device_id=((lat_at + turn + n_lat) % n_lat, lon_at),
            )

    def side_copies(begin):
        for up, climb in enumerate((1, 0, -1)):
            for side, turn in enumerate((1, -1)):
                exchange_pair(
                    begin, *lat_has(n_lat, lat_at, climb),
                    src_ref=side_strips.at[side],
                    dst_ref=near_sides.at[up, side],
                    send_sem=side_send.at[up * 2 + side], recv_sem=side_recv.at[up * 2 + side],
                    device_id=((lat_at + climb + n_lat) % n_lat, lon_peer(turn)),
                )

    def prepare():
        make_operators(n_lat, rows, cells, each, lat_taps, lon_taps, lat_op, lon_op, edge_op)
        make_strips(ens, side_strips)

    number = 3
    for iteration in range(iterations):
        before = iteration - 1
        if iteration > 0:
            around = field.at[before]
            for k in range(n_lat):
                a = lat_peer(k)
                for at, turn in enumerate((1, 0, -1)):
                    if k == 0 and turn == 0:
                        continue
                    copy_to(
                        held.at[of_task(a)], around.at[at * n_lat + lat_at], number,
                        (a, lon_peer(turn)),
                    ).start()
            field[before, n_lat + lat_at] = held[of_task(lat_at)]
            if iteration == 1:
                wait(whole, 1, n_lat - 1)
                wait(near_strips, 2, 2 * n_lat)
            wait(around, number, 3 * n_lat - 1)
            if iteration == 1:
                near_chunk(0, True)
                side_copies(True)
            covariance(
                HYBRID_ENSEMBLE**2 / (members - 1),
                [HYBRID_STATIC**2 * sigma[lat_at * task + l] ** 2 for l in range(task)],
                whole, near_strips.reshape(2, n_lat, *near_strips.shape[1:]), around,
                lat_op, lon_op, edge_op, edge, part,
            )
            home = part_in.at[before]
            for k in range(1, n_lat):
                a = lat_peer(k)
                copy_to(part.at[a], home.at[lat_at], number + 1, (a, lon_at)).start()
            part_in[before, lat_at] = part[lat_at]
            wait(home, number + 1, n_lat - 1)
            if iteration == 1:
                near_chunk(1, True)
            to_slots(cols, part_in[before].reshape(levels, rows, cells), packed)
            exchange(
                packed, table.at[before], number + 2,
                functools.partial(
                    make_adjoint_operators, rows, each, members // side_strips.shape[1], cells, lat_taps, lon_taps,
                    lat_adjoint, lon_adjoint, edge_adjoint,
                ) if iteration == 1 else None,
            )
            number += 3
            if iteration == 1:
                near_chunk(2, True)
                near_chunk(3, True)
        obs_step(
            table.at[before] if iteration > 0 else None,
            hi, lo, weight, innov, prec, departure, pushed, devices * levels, slots,
        )
        exchange(
            pushed, incoming.at[iteration], number,
            prepare if iteration == 0 else None,
        )
        number += 1
        forcing = to_columns(cols, incoming.at[iteration], held.shape)
        if iteration == 0:
            held[...] = -step[0] * forcing
        else:
            held[...] = held[...] - step[iteration] * (forcing + held[...])

    held_copies(n_lat, n_lon, lat_at, lon_at, held, near_held, held_send, held_recv, True)
    near_held[1, 1] = held[...]
    for chunk in range(CHUNKS):
        near_chunk(chunk, False)
    side_copies(False)
    held_copies(n_lat, n_lon, lat_at, lon_at, held, near_held, held_send, held_recv, False)


def exchange_pair(begin, has_send, has_recv, **copy):
    made = pltpu.make_async_remote_copy(device_id_type=MESH, **copy)
    if begin:
        pl.when(has_send)(made.start)
    else:
        pl.when(has_send)(made.wait_send)
        pl.when(has_recv)(made.wait_recv)


def lat_has(n_lat, lat_at, step):
    send = jnp.logical_and(lat_at + step >= 0, lat_at + step < n_lat)
    recv = jnp.logical_and(lat_at - step >= 0, lat_at - step < n_lat)
    return send, recv


def held_copies(n_lat, n_lon, lat_at, lon_at, held, near_held, held_send, held_recv, begin):
    for up, step in enumerate((1, 0, -1)):
        has = lat_has(n_lat, lat_at, step)
        for side, turn in enumerate((1, 0, -1)):
            if step == 0 and turn == 0:
                continue
            exchange_pair(
                begin, *has,
                src_ref=held, dst_ref=near_held.at[up, side],
                send_sem=held_send.at[up * 3 + side], recv_sem=held_recv.at[up * 3 + side],
                device_id=((lat_at + step + n_lat) % n_lat, (lon_at + turn + n_lon) % n_lon),
            )


def adjoint_kernel(
    scale, n_lat,
    sigma, members, near, sides, field, lon_op, lat_op, edge_op, departure,
    out, static_out, departure_out,
    own, edge_field, edge,
):
    batch, levels, rows, cells = out.shape
    groups = sides.shape[2]
    each = lat_op.shape[0] // (2 * rows)
    packed = edge_op.shape[2] // cells
    width = cells // packed
    lat_at = lax.axis_index("lat")
    keep = (lat_at > 0, None, lat_at < n_lat - 1)
    lon_high, lon_low = lon_op[0], lon_op[1]
    size = lat_op.shape[0] // 2

    def kept(part, value):
        return value if keep[part] is None else jnp.where(keep[part], value, 0.0)

    def along_lat(stacked):
        high, low = halves(stacked)
        both = dot(lat_op[...], high)
        return both[:size] + both[size:] + dot(lat_op[:size], low)

    def along_lon(stacked):
        high, low = halves(stacked)
        return dot(high, lon_high) + dot(high, lon_low) + dot(low, lon_high)

    @pl.when(pl.program_id(0) == 0)
    def _():
        departure_out[...] = departure[...]
        for part in range(3):
            own[part] = kept(part, field[part, 1])
            for side in range(2):
                value = kept(part, field[part, 2 * side]).reshape(levels * rows, cells)
                high, low = halves(value)
                tile = pick(width, None, side, cells)
                edge_field[part, side] = (dot(high, tile) + dot(low, tile)).reshape(
                    levels, rows, cells
                )

        def edge_of(group):
            results = []
            for first in range(0, levels, each):
                pieces = []
                for part in range(3):
                    lanes = []
                    for side in range(2):
                        value = edge_field[part, side, first : first + each]
                        if group is not None:
                            some = sides[part, side, group, first : first + each].astype(F32)
                            value = kept(part, some * value)
                        lanes.append(value.reshape(size, cells))
                    pieces.append(jnp.concatenate(lanes, axis=1))
                results.append(along_lat(jnp.concatenate(pieces, axis=0)))
            return results

        stacked = jnp.concatenate(
            [piece for g in list(range(groups)) + [None] for piece in edge_of(g)], axis=0
        )
        high, low = halves(stacked)
        edge[...] = (
            dot(high, edge_op[0]) + dot(high, edge_op[1]) + dot(low, edge_op[0])
        ).reshape(edge.shape)
        results = []
        for first in range(0, levels, each):
            stacked = jnp.concatenate(
                [own[part, first : first + each].reshape(size, cells) for part in range(3)], axis=0
            )
            both = jnp.concatenate([stacked, jnp.zeros_like(stacked)], axis=1)
            results.append(along_lat(both))
        smooth = along_lon(jnp.concatenate(results, axis=0))[:, :cells].reshape(
            levels, rows, cells
        )
        for l in range(levels):
            static_out[l] = (HYBRID_STATIC * sigma[l]) * (
                smooth[l] + edge[groups, l, :, :cells]
            )

    for g in range(batch // each):
        some = pl.ds(g * each, each)
        group = pl.program_id(0) * (batch // packed) + g * each // packed
        spot = g * each % packed
        results = []
        for first in range(0, levels, 2):
            pieces = []
            for part in range(3):
                lanes = []
                for l in range(first, min(first + 2, levels)):
                    values = members[some, l] if part == 1 else near[part // 2, some, l]
                    lanes.append(
                        kept(part, values.astype(F32) * own[part, l][None]).reshape(size, cells)
                    )
                if len(lanes) == 1:
                    lanes.append(jnp.zeros((size, cells), F32))
                pieces.append(jnp.concatenate(lanes, axis=1))
            results.append(along_lat(jnp.concatenate(pieces, axis=0)))
        smooth = along_lon(jnp.concatenate(results, axis=0))
        for l in range(levels):
            block = smooth[l // 2 * size : (l // 2 + 1) * size]
            block = block[:, l % 2 * cells : (l % 2 + 1) * cells].reshape(each, rows, cells)
            extra = jnp.stack(
                [
                    edge[group, l, :, j * cells : (j + 1) * cells]
                    for j in range(spot, spot + each)
                ], axis=0
            )
            out[some, l] = scale * (block + extra)


def divisor(count, limit):
    return max(n for n in range(1, count + 1) if count % n == 0 and (n <= limit or n == 1))


def per_device(
    ensemble,
    static_sigma,
    lat_taps,
    lon_taps,
    step_len,
    send_cols,
    send_count,
    obs_ref,
    obs_level,
    obs_weight,
    innovation,
    obs_precision,
):
    members, levels, rows, cells = ensemble.shape
    half = (lat_taps.shape[0] - 1) // 2
    n_lat, n_lon = lax.axis_size("lat"), lax.axis_size("lon")
    devices = n_lat * n_lon
    slots = send_cols.shape[3]
    scale = HYBRID_ENSEMBLE / math.sqrt(members - 1)

    positions = obs_ref.reshape(obs_ref.shape[2], -1)
    weight = obs_weight.reshape(positions.shape)
    task = levels // n_lat
    each = cells // (2 * half)
    groups = members // each
    assert task * n_lat == levels and each * 2 * half == cells and groups * each == members
    assert levels % each == 0

    wide_slots = max(slots, 256)
    cols = send_cols.reshape(-1, wide_slots)
    iterations = step_len.shape[0]
    some = divisor(each, max(1, 256 // (n_lat * rows)))
    lat_size = n_lat * rows * some
    later = max(1, iterations - 1)
    count_width = -(-devices // 128) * 128
    smem = pl.BlockSpec(memory_space=pltpu.SMEM)
    hbm = pl.BlockSpec(memory_space=pl.ANY)
    exchanges = 3 + iterations + 3 * (iterations - 1)
    strip = (groups, levels, rows, cells)
    narrow = slots % LANES == 0 and levels == 8 and slots // LANES * levels % 16 == 0
    block = (devices, slots // LANES * levels, LANES)
    lat_shape = (2 * each * rows, 3 * each * rows)
    pair_shape = (2, 2 * cells, 2 * cells)
    edge_shape = (2, 2 * cells, each * cells)
    packed = 2 * each
    side_strip = (members // packed, levels, rows, cells)
    side_shape = (2, 2 * cells, packed * cells)
    assert members % packed == 0
    departure, near, near_sides, near_held, lat_adjoint, lon_adjoint, edge_adjoint = pl.pallas_call(
        functools.partial(main_kernel, n_lat, n_lon, iterations, narrow),
        out_shape=(
            jax.ShapeDtypeStruct((1, positions.shape[1]), F32),
            jax.ShapeDtypeStruct((2,) + ensemble.shape, BF16),
            jax.ShapeDtypeStruct((3, 2) + side_strip, BF16),
            jax.ShapeDtypeStruct((3, 3, levels, rows, cells), F32),
            jax.ShapeDtypeStruct(lat_shape, BF16),
            jax.ShapeDtypeStruct(pair_shape, BF16),
            jax.ShapeDtypeStruct(side_shape, BF16),
        ),
        in_specs=[smem] * 4 + [hbm] * 8,
        out_specs=(VMEM, hbm, VMEM, VMEM, VMEM, VMEM, VMEM),
        scratch_shapes=[
            pltpu.VMEM((1, count_width), jnp.int32),
            pltpu.VMEM((devices, 1, count_width), jnp.int32),
            pltpu.VMEM((n_lat, members, task, rows, cells), BF16),
            pltpu.VMEM((2,) + strip, BF16),
            pltpu.VMEM((2,) + side_strip, BF16),
            pltpu.VMEM((2 * n_lat, groups, task, rows, cells), BF16),
            pltpu.VMEM((devices, levels, slots), F32),
            pltpu.VMEM((iterations, devices, levels, slots), F32),
            pltpu.VMEM((levels, rows, cells), F32),
            pltpu.VMEM((later, 3 * n_lat, task, rows, cells), F32),
            pltpu.VMEM((n_lat, task, rows, cells), F32),
            pltpu.VMEM((later, n_lat, task, rows, cells), F32),
            pltpu.VMEM((devices, levels, slots), F32),
            pltpu.VMEM((later, devices, levels, slots), F32),
        ]
        + ([pltpu.VMEM(block, jnp.int16), pltpu.VMEM((exchanges - 3,) + block, jnp.int16)] if narrow else [])
        + [
            pltpu.VMEM(positions.shape, jnp.int32),
            pltpu.VMEM(positions.shape, jnp.int32),
            pltpu.VMEM((2 * lat_size, lat_size), BF16),
            pltpu.VMEM(pair_shape, BF16),
            pltpu.VMEM(edge_shape, BF16),
            pltpu.VMEM((n_lat, groups + 1, task, rows, each * cells), F32),
            pltpu.VMEM(ensemble.shape, BF16),
            pltpu.VMEM((1, devices), jnp.int32),
            pltpu.VMEM(cols.shape, jnp.int32),
            pltpu.VMEM(positions.shape, jnp.int32),
            pltpu.VMEM((1, positions.shape[1]), jnp.int32),
            pltpu.VMEM(positions.shape, F32),
            pltpu.VMEM((1, positions.shape[1]), F32),
            pltpu.VMEM((1, positions.shape[1]), F32),
            pltpu.SemaphoreType.DMA((exchanges,)),
            pltpu.SemaphoreType.DMA((exchanges,)),
            pltpu.SemaphoreType.DMA((2 * CHUNKS,)),
            pltpu.SemaphoreType.DMA((2 * CHUNKS,)),
            pltpu.SemaphoreType.DMA((6,)),
            pltpu.SemaphoreType.DMA((6,)),
            pltpu.SemaphoreType.DMA((9,)),
            pltpu.SemaphoreType.DMA((9,)),
            pltpu.SemaphoreType.DMA((8,)),
        ],
        compiler_params=pltpu.CompilerParams(
            collective_id=0, has_side_effects=True, vmem_limit_bytes=VMEM_LIMIT
        ),
        name="analysis",
    )(
        static_sigma, step_len, lat_taps, lon_taps, ensemble, send_count.reshape(1, -1), cols,
        positions, obs_level.reshape(1, -1), weight, innovation.reshape(1, -1),
        obs_precision.reshape(1, -1),
    )
    batch = packed
    own_spec = pl.BlockSpec((batch, levels, rows, cells), lambda k: (k, 0, 0, 0))
    near_spec = pl.BlockSpec((2, batch, levels, rows, cells), lambda k: (0, k, 0, 0, 0))
    control, static, departure = pl.pallas_call(
        functools.partial(adjoint_kernel, scale, n_lat),
        grid=(members // batch,),
        out_shape=(
            jax.ShapeDtypeStruct(ensemble.shape, F32),
            jax.ShapeDtypeStruct((levels, rows, cells), F32),
            jax.ShapeDtypeStruct(departure.shape, F32),
        ),
        in_specs=[smem, own_spec, near_spec] + [VMEM] * 6,
        out_specs=(
            pl.BlockSpec((batch, levels, rows, cells), lambda k: (k, 0, 0, 0)),
            pl.BlockSpec((levels, rows, cells), lambda k: (0, 0, 0)),
            pl.BlockSpec(departure.shape, lambda k: (0, 0)),
        ),
        scratch_shapes=[
            pltpu.VMEM((3, levels, rows, cells), F32),
            pltpu.VMEM((3, 2, levels, rows, cells), F32),
            pltpu.VMEM((members // packed + 1, levels, rows, packed * cells), F32),
        ],
        compiler_params=pltpu.CompilerParams(vmem_limit_bytes=VMEM_LIMIT),
        name="adjoint",
    )(
        static_sigma, ensemble, near, near_sides, near_held, lon_adjoint, lat_adjoint,
        edge_adjoint, departure,
    )
    return control, static, departure.reshape(1, 1, -1)


def solution(mesh):
    return jax.shard_map(
        per_device,
        mesh=mesh,
        in_specs=(
            P(None, None, "lat", "lon"),
            P(),
            P(),
            P(),
            P(),
            P("lat", "lon", None, None),
            P("lat", "lon", None),
            P("lat", "lon", None, None),
            P("lat", "lon", None),
            P("lat", "lon", None, None),
            P("lat", "lon", None),
            P("lat", "lon", None),
        ),
        out_specs=(P(None, None, "lat", "lon"), P(None, "lat", "lon"), P("lat", "lon", None)),
        check_vma=False,
    )
```

```python
import functools
import math

import jax
import jax.numpy as jnp
from jax import lax
from jax.experimental import pallas as pl
from jax.experimental.pallas import tpu as pltpu
from jax.sharding import PartitionSpec as P

HYBRID_STATIC = 0.5
HYBRID_ENSEMBLE = 0.8660254037844386
BF16 = jnp.bfloat16
F32 = jnp.float32
MESH = pl.DeviceIdType.MESH
LANES = 128
STEPS = 16383.0
VMEM_LIMIT = 60 * 2**20
VMEM = pl.BlockSpec(memory_space=pltpu.VMEM)


def halves(x):
    high = x.astype(BF16)
    return high, (x - high.astype(F32)).astype(BF16)


def dot(a, b):
    return jnp.dot(a, b, preferred_element_type=F32)


def dot_nt(a, b):
    return lax.dot_general(a, b, (((1,), (1,)), ((), ())), preferred_element_type=F32)


def dot3(a, b):
    a_high, a_low = halves(a)
    b_high, b_low = halves(b)
    return dot(a_high, b_high) + dot(a_high, b_low) + dot(a_low, b_high)


def iota(shape, dim):
    return lax.broadcasted_iota(jnp.int32, shape, dim)


def obs_step(table, hi, lo, weight, innov, prec, departure, out, rows, slots):
    chunk = 2048 if rows <= 256 else 256
    points = hi.shape[0]
    if table is not None:
        table_both = jnp.concatenate(halves(table[...].reshape(rows, slots)), axis=0)

    def step(index, carry):
        where = pl.ds(pl.multiple_of(index * chunk, chunk), chunk)
        row_ids = iota((rows, chunk), 0)
        slot_ids = iota((slots, chunk), 0)
        value = -innov[:, where]
        if table is not None:
            for q in range(points):
                lo_hot = jnp.where(slot_ids == lo[q : q + 1, where], 1.0, 0.0).astype(BF16)
                product = dot(table_both, lo_hot)
                product = product[:rows] + product[rows:]
                picked = jnp.sum(
                    jnp.where(row_ids == hi[q : q + 1, where], product, 0.0), axis=0, keepdims=True
                )
                value = value + weight[q : q + 1, where] * picked
            departure[:, where] = value
        value = prec[:, where] * value
        total = None
        for q in range(points):
            lo_hot = jnp.where(slot_ids == lo[q : q + 1, where], 1.0, 0.0).astype(BF16)
            pushed = weight[q : q + 1, where] * value
            high = pushed.astype(BF16).astype(F32)
            chosen = row_ids == hi[q : q + 1, where]
            both = jnp.concatenate(
                [jnp.where(chosen, high, 0.0), jnp.where(chosen, pushed - high, 0.0)], axis=0
            ).astype(BF16)
            term = dot_nt(both, lo_hot)
            term = term[:rows] + term[rows:]
            total = term if total is None else total + term
        return carry + total

    total = lax.fori_loop(0, hi.shape[1] // chunk, step, jnp.zeros((rows, slots), F32))
    out[...] = total.reshape(out.shape)


def encode(values, out):
    devices, levels, slots = values.shape
    lane = iota((devices, levels, LANES), 2)
    codes = []
    for first in range(0, slots, LANES):
        value = values[:, :, first : first + LANES]
        top = jnp.max(jnp.abs(value), axis=2, keepdims=True)
        power = jnp.clip(jnp.ceil(jnp.log2(jnp.maximum(top, 1e-30))), -99.0, 120.0)
        value = jnp.clip(jnp.floor(value * (STEPS * jnp.exp2(-power)) + 0.5), -STEPS, STEPS)
        shift = jnp.broadcast_to(power.astype(jnp.int32) + 128, lane.shape)
        bit = jnp.bitwise_and(jnp.right_shift(shift, jnp.bitwise_and(lane, 7)), 1)
        codes.append(2 * value.astype(jnp.int32) + bit)
    out[...] = jnp.concatenate(codes, axis=1).astype(jnp.int16)


def decode(coded, out):
    devices, levels, slots = out.shape
    code = coded[...].astype(jnp.int32)
    for piece in range(slots // LANES):
        some = code[:, piece * levels : (piece + 1) * levels]
        bit = jnp.bitwise_and(some, 1).astype(F32).reshape(devices * levels, LANES)
        row = iota((LANES, LANES), 0)
        worth = jnp.where(row < 8, jnp.exp2(row.astype(F32)), 0.0).astype(BF16)
        power = dot(bit.astype(BF16), worth).reshape(some.shape) - 128.0
        value = jnp.right_shift(some, 1).astype(F32) * (jnp.exp2(power) * (1.0 / STEPS))
        out[:, :, piece * LANES : (piece + 1) * LANES] = value


def cell_and_row(col, cells):
    if cells & (cells - 1):
        return col % cells, col // cells
    return jnp.bitwise_and(col, cells - 1), jnp.right_shift(col, cells.bit_length() - 1)


def split(ids, size):
    inner, outer = cell_and_row(ids, size)
    return outer, inner


def to_slots(cols, field, out):
    levels, lat_rows, cells = field.shape
    slots = out.shape[2]
    width = cols.shape[1]
    per_row = width // slots
    rows = jnp.concatenate([field[:, r, :] for r in range(lat_rows)], axis=0)
    count = rows.shape[0]
    both = jnp.concatenate(halves(rows), axis=0)

    def step(index, carry):
        col = cols[pl.ds(index, 1), :]
        cell, at_row = cell_and_row(col, cells)
        cell_hot = jnp.where(iota((cells, width), 0) == cell, 1.0, 0.0).astype(BF16)
        product = dot(both, cell_hot)
        product = product[:count] + product[count:]
        row = jnp.broadcast_to(at_row, (levels, width))
        total = jnp.zeros((levels, width), F32)
        for r in range(lat_rows):
            total = jnp.where(row == r, product[r * levels : (r + 1) * levels], total)
        for j in range(per_row):
            out[index * per_row + j] = total[:, j * slots : (j + 1) * slots]
        return carry

    lax.fori_loop(0, cols.shape[0], step, 0, unroll=4)


def to_columns(cols, values, shape):
    levels, lat_rows, cells = shape
    slots = values.shape[2]
    width = cols.shape[1]
    per_row = width // slots
    count = levels * lat_rows

    def step(index, total):
        col = cols[pl.ds(index, 1), :]
        cell, at_row = cell_and_row(col, cells)
        cell_hot = jnp.where(iota((cells, width), 0) == cell, 1.0, 0.0).astype(BF16)
        chosen = iota((lat_rows, width), 0) == at_row
        value = values[index * per_row]
        if per_row > 1:
            value = jnp.concatenate(
                [values[index * per_row + j] for j in range(per_row)], axis=1
            )
        high = value.astype(BF16).astype(F32)
        low = value - high
        parts = [jnp.where(chosen, high[l : l + 1], 0.0) for l in range(levels)]
        parts += [jnp.where(chosen, low[l : l + 1], 0.0) for l in range(levels)]
        return total + dot_nt(jnp.concatenate(parts, axis=0).astype(BF16), cell_hot)

    total = lax.fori_loop(
        0, cols.shape[0], step, jnp.zeros((2 * count, cells), F32), unroll=4
    )
    return (total[:count] + total[count:]).reshape(shape)


def pick(width, group, side, cells):
    row, col = iota((cells, cells), 0), iota((cells, cells), 1)
    member, spot = split(col, width)
    here = row == (spot if side else spot + (cells - width))
    if group is not None:
        here = jnp.logical_and(here, member == group)
    return jnp.where(here, 1.0, 0.0).astype(BF16)


def make_strips(ens, strips):
    _, groups, levels, rows, cells = strips.shape
    each = ens.shape[0] // groups
    width = cells // each
    total = None
    for j in range(each):
        some = jnp.concatenate([ens[g * each + j] for g in range(groups)], axis=0)
        some = some.reshape(groups * levels * rows, cells)
        both = jnp.concatenate([pick(width, j, 0, cells), pick(width, j, 1, cells)], axis=1)
        term = dot(some, both)
        total = term if total is None else total + term
    for side in range(2):
        strips[side] = (
            total[:, side * cells : (side + 1) * cells].astype(BF16).reshape(strips.shape[1:])
        )


def covariance(ens_coef, static_coef, whole, strips, field, lat_op, lon_op, edge_op, edge, out, first, arrive):
    n_lat, members, levels, rows, cells = whole.shape
    groups = strips.shape[2]
    each = members // groups
    some = lat_op.shape[1] // (n_lat * rows)
    parts = each // some
    size = n_lat * some * rows
    width = cells // each
    edge_high, edge_low = edge_op[0], edge_op[1]
    sides = []
    for side in range(2):
        block = field[2 * side * n_lat : (2 * side + 1) * n_lat]
        high, low = halves(block.reshape(n_lat * levels * rows, cells))
        tile = pick(width, None, side, cells)
        sides.append((dot(high, tile) + dot(low, tile)).reshape(n_lat, levels, rows, cells))
    for a in range(n_lat):
        wide = []
        for side in range(2):
            h = sides[side][a]
            terms = (strips[side, a].astype(F32) * h[None]).reshape(groups * levels * rows, cells)
            wide.append(jnp.concatenate([terms, h.reshape(levels * rows, cells)], axis=0))
        high, low = halves(jnp.concatenate(wide, axis=1))
        edge[a] = (
            dot(high, edge_high) + dot(high, edge_low) + dot(low, edge_high)
        ).reshape(edge.shape[1:])
    lon_high, lon_low = lon_op[0], lon_op[1]

    def smooth(pieces, group, width_of):
        lanes = []
        for index, (l, p, piece) in enumerate(pieces):
            lanes.append(piece.reshape(size, cells))
        count = len(lanes)
        if count % 2:
            lanes.append(jnp.zeros((size, cells), F32))
        results = []
        for first in range(0, count, 2):
            high, low = halves(jnp.concatenate(lanes[first : first + 2], axis=1))
            mid = dot(high, lon_high) + dot(high, lon_low) + dot(low, lon_high)
            extra = []
            for l, p, piece in pieces[first : first + 2]:
                at = [width_of(p * some + j) for j in range(some)]
                extra.append(
                    jnp.stack(
                        [edge[:, group, l, :, x * cells : (x + 1) * cells] for x in at], axis=1
                    ).reshape(size, cells)
                )
            if len(extra) == 1:
                extra.append(jnp.zeros((size, cells), F32))
            high, low = halves(mid + jnp.concatenate(extra, axis=1))
            both = dot(lat_op[...], high)
            done = both[:size] + both[size:] + dot(lat_op[:size], low)
            for index in range(min(2, count - first)):
                results.append(
                    done[:, index * cells : (index + 1) * cells].reshape(n_lat, some, rows, cells)
                )
        return results

    own = [field[n_lat : 2 * n_lat, l] for l in range(levels)]

    def step(group, total):
        pieces, kept = [], []
        for l in range(levels):
            for p in range(parts):
                values = whole[:, pl.ds(group * each + p * some, some), l].astype(F32)
                kept.append((l, values))
                pieces.append((l, p, values * own[l][:, None]))
        done = smooth(pieces, group, lambda x: x)
        total = list(total)
        for (l, values), result in zip(kept, done):
            total[l] = total[l] + jnp.sum(values * result, axis=1)
        return tuple(total)

    zero = jnp.zeros((n_lat, rows, cells), F32)
    total = lax.fori_loop(0, first, step, (zero,) * levels)
    if arrive is not None:
        arrive()
    total = lax.fori_loop(first, groups, step, total)
    pieces = []
    for l in range(levels):
        piece = [own[l]] + [zero] * (some - 1)
        pieces.append((l, 0, jnp.stack(piece, axis=1)))
    done = smooth(pieces, groups, lambda x: 0)
    for l in range(levels):
        out[:, l] = ens_coef * total[l] + static_coef[l] * done[l][:, 0]


def banded(taps, offset):
    total = jnp.zeros(offset.shape, F32)
    for t in range(len(taps)):
        total = jnp.where(offset == t, taps[t], total)
    return total


def store_halves(ref, value):
    ref[0], ref[1] = halves(value)


def edge_operator(taps, reach, each, cells, op):
    width = cells // each
    row, col = iota((2 * cells, cells), 0), iota((2 * cells, cells), 1)
    side, lane = split(row, cells)
    member, spot = split(lane, width)
    at = jnp.where(side == 0, spot - width, spot + cells)
    value = banded(taps, at - col + reach)
    for j in range(each):
        high, low = halves(jnp.where(member == j, value, 0.0))
        op[0, :, j * cells : (j + 1) * cells] = high
        op[1, :, j * cells : (j + 1) * cells] = low


def pair_operator(taps, reach, cells, op):
    row, col = iota((2 * cells, 2 * cells), 0), iota((2 * cells, 2 * cells), 1)
    row_block, row_at = split(row, cells)
    col_block, col_at = split(col, cells)
    store_halves(
        op, jnp.where(row_block == col_block, banded(taps, row_at - col_at + reach), 0.0)
    )


def make_operators(n_lat, rows, cells, each, lat_taps, lon_taps, lat_op, lon_op, edge_op):
    count = lat_taps.shape[0]
    half = (count - 1) // 2
    lat = [lat_taps[t] for t in range(count)]
    lon = [lon_taps[t] for t in range(count)]
    size = lat_op.shape[1]
    some = size // (n_lat * rows)
    row, col = iota((size, size), 0), iota((size, size), 1)

    def lat_of(ids):
        outer, r = split(ids, rows)
        a, j = split(outer, some)
        return a * rows + r, j

    row_at, row_member = lat_of(row)
    col_at, col_member = lat_of(col)
    high, low = halves(
        jnp.where(row_member == col_member, banded(lat, col_at - row_at + half), 0.0)
    )
    lat_op[:size], lat_op[size:] = halves(
        dot_nt(high, high) + dot_nt(high, low) + dot_nt(low, high)
    )
    corr = []
    for lag in range(-2 * half, 2 * half + 1):
        terms = [lon[t] * lon[t - lag] for t in range(count) if 0 <= t - lag < count]
        corr.append(functools.reduce(lambda a, b: a + b, terms))
    pair_operator(corr, 2 * half, cells, lon_op)
    edge_operator(corr, 2 * half, each, cells, edge_op)


def make_adjoint_operators(rows, each, packed, cells, lat_taps, lon_taps, lat_op, lon_op, edge_op):
    count = lat_taps.shape[0]
    half = (count - 1) // 2
    lat = [lat_taps[t] for t in range(count)][::-1]
    lon = [lon_taps[t] for t in range(count)][::-1]
    shape = (each * rows, 3 * each * rows)
    row_member, row_at = split(iota(shape, 0), rows)
    outer, col_at = split(iota(shape, 1), rows)
    part, col_member = split(outer, each)
    offset = (part - 1) * rows + col_at - row_at + half
    lat_op[: shape[0]], lat_op[shape[0] :] = halves(
        jnp.where(row_member == col_member, banded(lat, offset), 0.0)
    )
    pair_operator(lon, half, cells, lon_op)
    edge_operator(lon, half, packed, cells, edge_op)


def main_kernel(n_lat, n_lon, iterations, narrow, *refs):
    if not narrow:
        at = 33
        refs = refs[:at] + (None, None) + refs[at:]
    main_body(n_lat, n_lon, iterations, *refs)


def main_body(
    n_lat, n_lon, iterations,
    sigma, step, lat_taps, lon_taps, ens_far, count_far, cols_far, pos_far, level_far, weight_far,
    innov_far, prec_far,
    departure, near, near_sides, near_held, lat_adjoint, lon_adjoint, edge_adjoint,
    count_row, counts, whole, strips, side_strips, near_strips, pushed, incoming, held, field, part, part_in,
    packed, table, coded, arrived, hi, lo, lat_op, lon_op, edge_op, edge,
    ens, send_count, cols, pos, level, weight, innov, prec,
    ex_send, ex_recv, near_send, near_recv, side_send, side_recv, held_send, held_recv, load_sem, own_sem,
):
    lat_at, lon_at = lax.axis_index("lat"), lax.axis_index("lon")
    me = lat_at * n_lon + lon_at
    devices = n_lat * n_lon
    levels, rows, cells = held.shape
    slots = pushed.shape[2]
    members = ens.shape[0]
    task = levels // n_lat
    each = members // strips.shape[1]

    def place(d):
        return (d // n_lon, d % n_lon)

    barrier = pltpu.get_barrier_semaphore()

    def greet(k, carry):
        pl.semaphore_signal(
            barrier, inc=1, device_id=place((me + k) % devices), device_id_type=MESH
        )
        return carry

    lax.fori_loop(1, devices, greet, 0)
    loads = [
        pltpu.make_async_copy(far, here, load_sem.at[index])
        for index, (far, here) in enumerate(
            (
                (count_far, send_count), (ens_far, ens), (pos_far, pos), (level_far, level),
                (weight_far, weight), (innov_far, innov), (prec_far, prec), (cols_far, cols),
            )
        )
    ]
    for load in loads:
        load.start()
    count_row[...] = jnp.zeros_like(count_row)
    loads[0].wait()
    count_row[:, :devices] = send_count[...]
    make_operators(n_lat, rows, cells, each, lat_taps, lon_taps, lat_op, lon_op, edge_op)
    pl.semaphore_wait(barrier, devices - 1)

    def copy_to(source, target, number, device):
        return pltpu.make_async_remote_copy(
            src_ref=source, dst_ref=target, send_sem=ex_send.at[number],
            recv_sem=ex_recv.at[number], device_id=device, device_id_type=MESH,
        )

    def send(source, target, number):
        def one(k, carry):
            d = (me + k) % devices
            copy_to(source(d), target.at[me], number, place(d)).start()
            return carry

        lax.fori_loop(1, devices, one, 0)

    def wait(target, number, count=devices - 1):
        every = target.at[pl.ds(0, count)]
        copy = copy_to(every, every, number, place((me + 1) % devices))
        copy.wait_send()
        copy.wait_recv()

    def exchange(values, target, number, meanwhile=None):
        if coded is None:
            send(lambda d: values.at[d], target, number)
            target[me] = values[me]
        else:
            index = number - 3
            encode(values, coded)
            send(lambda d: coded.at[d], arrived.at[index], number)
            arrived[index, me] = coded[me]
        if meanwhile is not None:
            meanwhile()
        if coded is None:
            wait(target, number)
        else:
            wait(arrived.at[index], number)
            decode(arrived.at[index], target)

    def of_task(a):
        return pl.ds(a * task, task)

    def lat_peer(k):
        return (lat_at + k) % n_lat

    def lon_peer(turn):
        return (lon_at + turn + n_lon) % n_lon

    send(lambda d: count_row, counts, 0)
    counts[me] = count_row[...]
    early = strips.shape[1] * 1 // 2 * each
    halves_of = (pl.ds(0, early), pl.ds(early, members - early))

    def spread(index):
        some = halves_of[index]
        for k in range(1, n_lat):
            a = lat_peer(k)
            copy_to(
                ens_far.at[some, of_task(a)], whole.at[lat_at, some],
                ex_send.shape[0] - 1 if index else 1, (a, lon_at),
            ).start()

    def spread_wait(index):
        every = whole.at[pl.ds(0, n_lat - 1), halves_of[index]]
        copy = copy_to(
            every, every, ex_send.shape[0] - 1 if index else 1, place((me + 1) % devices)
        )
        copy.wait_send()
        copy.wait_recv()

    spread(0)
    loads[1].wait()
    whole[lat_at] = ens[:, of_task(lat_at)]
    make_strips(ens, strips)
    for k in range(n_lat):
        a = lat_peer(k)
        for side, turn in enumerate((1, -1)):
            copy_to(
                strips.at[side, :, of_task(a)], near_strips.at[side * n_lat + lat_at], 2,
                (a, lon_peer(turn)),
            ).start()
    for load in loads[2:]:
        load.wait()
    wait(counts, 0)
    received = jnp.concatenate([counts[d] for d in range(devices)], axis=0)
    width = received.shape[1]
    column = jnp.sum(
        jnp.where(iota((devices, width), 1) == me, received, 0), axis=1, keepdims=True
    )
    as_row = jnp.sum(
        jnp.where(iota((devices, width), 0) == iota((devices, width), 1), column, 0),
        axis=0, keepdims=True,
    )
    ends = jnp.sum(
        jnp.where(iota((devices, width), 1) <= iota((devices, width), 0), as_row, 0),
        axis=1, keepdims=True,
    )
    for q in range(pos.shape[0]):
        place_q = pos[q : q + 1, :]
        past = place_q >= ends
        source = jnp.sum(jnp.where(past, 1, 0), axis=0, keepdims=True)
        lo[q : q + 1, :] = place_q - jnp.sum(jnp.where(past, column, 0), axis=0, keepdims=True)
        hi[q : q + 1, :] = source * levels + level[...]

    def near_chunk(chunk, begin):
        for index, turn in enumerate((1, -1)):
            some = of_task((lat_at + turn + chunk + n_lat) % n_lat)
            mine = of_task((lat_at + chunk) % n_lat)
            has_send, has_recv = lat_has(n_lat, lat_at, turn)
            if chunk == 0:
                local = pltpu.make_async_copy(
                    whole.at[(lat_at - turn + n_lat) % n_lat], near.at[index, :, mine],
                    own_sem.at[index],
                )
                pl.when(has_recv)(local.start if begin else local.wait)
                continue
            number = index * n_lat + chunk
            if begin:
                sent = pltpu.make_async_remote_copy(
                    src_ref=ens_far.at[:, some], dst_ref=near.at[index, :, some],
                    send_sem=near_send.at[number], recv_sem=near_recv.at[number],
                    device_id=((lat_at + turn + n_lat) % n_lat, lon_at), device_id_type=MESH,
                )
                pl.when(has_send)(sent.start)
            else:
                sent = pltpu.make_async_remote_copy(
                    src_ref=ens_far.at[:, some], dst_ref=near.at[index, :, mine],
                    send_sem=near_send.at[number], recv_sem=near_recv.at[number],
                    device_id=((lat_at + turn + n_lat) % n_lat, lon_at), device_id_type=MESH,
                )
                pl.when(has_send)(sent.wait_send)
                pl.when(has_recv)(sent.wait_recv)

    def side_copies(begin):
        for up, climb in enumerate((1, 0, -1)):
            for side, turn in enumerate((1, -1)):
                exchange_pair(
                    begin, *lat_has(n_lat, lat_at, climb),
                    src_ref=side_strips.at[side],
                    dst_ref=near_sides.at[up, side],
                    send_sem=side_send.at[up * 2 + side], recv_sem=side_recv.at[up * 2 + side],
                    device_id=((lat_at + climb + n_lat) % n_lat, lon_peer(turn)),
                )

    def prepare():
        spread(1)
        make_strips(ens, side_strips)

    number = 3
    for iteration in range(iterations):
        before = iteration - 1
        if iteration > 0:
            around = field.at[before]
            for k in range(n_lat):
                a = lat_peer(k)
                for at, turn in enumerate((1, 0, -1)):
                    if k == 0 and turn == 0:
                        continue
                    copy_to(
                        held.at[of_task(a)], around.at[at * n_lat + lat_at], number,
                        (a, lon_peer(turn)),
                    ).start()
            field[before, n_lat + lat_at] = held[of_task(lat_at)]
            if iteration == 1:
                spread_wait(0)
                wait(near_strips, 2, 2 * n_lat)
            wait(around, number, 3 * n_lat - 1)
            if iteration == 1:
                side_copies(True)
            covariance(
                HYBRID_ENSEMBLE**2 / (members - 1),
                [HYBRID_STATIC**2 * sigma[lat_at * task + l] ** 2 for l in range(task)],
                whole, near_strips.reshape(2, n_lat, *near_strips.shape[1:]), around,
                lat_op, lon_op, edge_op, edge, part, early // each,
                functools.partial(spread_wait, 1) if iteration == 1 else None,
            )
            if iteration == 1:
                near_chunk(0, True)
                near_chunk(1, True)
            home = part_in.at[before]
            for k in range(1, n_lat):
                a = lat_peer(k)
                copy_to(part.at[a], home.at[lat_at], number + 1, (a, lon_at)).start()
            part_in[before, lat_at] = part[lat_at]
            wait(home, number + 1, n_lat - 1)
            if iteration == 1:
                for chunk in range(2, 2 + (n_lat - 2) // 2):
                    near_chunk(chunk, True)
            to_slots(cols, part_in[before].reshape(levels, rows, cells), packed)
            exchange(
                packed, table.at[before], number + 2,
                functools.partial(
                    make_adjoint_operators, rows, each, members // side_strips.shape[1], cells, lat_taps, lon_taps,
                    lat_adjoint, lon_adjoint, edge_adjoint,
                ) if iteration == 1 else None,
            )
            number += 3
            if iteration == 1:
                for chunk in range(2 + (n_lat - 2) // 2, n_lat):
                    near_chunk(chunk, True)
        obs_step(
            table.at[before] if iteration > 0 else None,
            hi, lo, weight, innov, prec, departure, pushed, devices * levels, slots,
        )
        exchange(
            pushed, incoming.at[iteration], number,
            prepare if iteration == 0 else None,
        )
        number += 1
        forcing = to_columns(cols, incoming.at[iteration], held.shape)
        if iteration == 0:
            held[...] = -step[0] * forcing
        else:
            held[...] = held[...] - step[iteration] * (forcing + held[...])

    held_copies(n_lat, n_lon, lat_at, lon_at, held, near_held, held_send, held_recv, True)
    near_held[1, 1] = held[...]
    for chunk in range(n_lat):
        near_chunk(chunk, False)
    side_copies(False)
    held_copies(n_lat, n_lon, lat_at, lon_at, held, near_held, held_send, held_recv, False)


def exchange_pair(begin, has_send, has_recv, **copy):
    made = pltpu.make_async_remote_copy(device_id_type=MESH, **copy)
    if begin:
        pl.when(has_send)(made.start)
    else:
        pl.when(has_send)(made.wait_send)
        pl.when(has_recv)(made.wait_recv)


def lat_has(n_lat, lat_at, step):
    send = jnp.logical_and(lat_at + step >= 0, lat_at + step < n_lat)
    recv = jnp.logical_and(lat_at - step >= 0, lat_at - step < n_lat)
    return send, recv


def held_copies(n_lat, n_lon, lat_at, lon_at, held, near_held, held_send, held_recv, begin):
    for up, step in enumerate((1, 0, -1)):
        has = lat_has(n_lat, lat_at, step)
        for side, turn in enumerate((1, 0, -1)):
            if step == 0 and turn == 0:
                continue
            exchange_pair(
                begin, *has,
                src_ref=held, dst_ref=near_held.at[up, side],
                send_sem=held_send.at[up * 3 + side], recv_sem=held_recv.at[up * 3 + side],
                device_id=((lat_at + step + n_lat) % n_lat, (lon_at + turn + n_lon) % n_lon),
            )


def adjoint_kernel(
    scale, n_lat,
    sigma, members, near, sides, field, lon_op, lat_op, edge_op, departure,
    out, static_out, departure_out,
    own, edge_field, edge,
):
    batch, levels, rows, cells = out.shape
    groups = sides.shape[2]
    each = lat_op.shape[0] // (2 * rows)
    packed = edge_op.shape[2] // cells
    width = cells // packed
    lat_at = lax.axis_index("lat")
    keep = (lat_at > 0, None, lat_at < n_lat - 1)
    lon_high, lon_low = lon_op[0], lon_op[1]
    size = lat_op.shape[0] // 2

    def kept(part, value):
        return value if keep[part] is None else jnp.where(keep[part], value, 0.0)

    def along_lat(stacked):
        high, low = halves(stacked)
        both = dot(lat_op[...], high)
        return both[:size] + both[size:] + dot(lat_op[:size], low)

    def along_lon(stacked):
        high, low = halves(stacked)
        return dot(high, lon_high) + dot(high, lon_low) + dot(low, lon_high)

    @pl.when(pl.program_id(0) == 0)
    def _():
        departure_out[...] = departure[...]
        for part in range(3):
            own[part] = kept(part, field[part, 1])
            for side in range(2):
                value = kept(part, field[part, 2 * side]).reshape(levels * rows, cells)
                high, low = halves(value)
                tile = pick(width, None, side, cells)
                edge_field[part, side] = (dot(high, tile) + dot(low, tile)).reshape(
                    levels, rows, cells
                )

        def edge_of(group):
            results = []
            for first in range(0, levels, each):
                pieces = []
                for part in range(3):
                    lanes = []
                    for side in range(2):
                        value = edge_field[part, side, first : first + each]
                        if group is not None:
                            some = sides[part, side, group, first : first + each].astype(F32)
                            value = kept(part, some * value)
                        lanes.append(value.reshape(size, cells))
                    pieces.append(jnp.concatenate(lanes, axis=1))
                results.append(along_lat(jnp.concatenate(pieces, axis=0)))
            return results

        stacked = jnp.concatenate(
            [piece for g in list(range(groups)) + [None] for piece in edge_of(g)], axis=0
        )
        high, low = halves(stacked)
        edge[...] = (
            dot(high, edge_op[0]) + dot(high, edge_op[1]) + dot(low, edge_op[0])
        ).reshape(edge.shape)
        results = []
        for first in range(0, levels, each):
            stacked = jnp.concatenate(
                [own[part, first : first + each].reshape(size, cells) for part in range(3)], axis=0
            )
            both = jnp.concatenate([stacked, jnp.zeros_like(stacked)], axis=1)
            results.append(along_lat(both))
        smooth = along_lon(jnp.concatenate(results, axis=0))[:, :cells].reshape(
            levels, rows, cells
        )
        for l in range(levels):
            static_out[l] = (HYBRID_STATIC * sigma[l]) * (
                smooth[l] + edge[groups, l, :, :cells]
            )

    for g in range(batch // each):
        some = pl.ds(g * each, each)
        group = pl.program_id(0) * (batch // packed) + g * each // packed
        spot = g * each % packed
        results = []
        for first in range(0, levels, 2):
            pieces = []
            for part in range(3):
                lanes = []
                for l in range(first, min(first + 2, levels)):
                    values = members[some, l] if part == 1 else near[part // 2, some, l]
                    lanes.append(
                        kept(part, values.astype(F32) * own[part, l][None]).reshape(size, cells)
                    )
                if len(lanes) == 1:
                    lanes.append(jnp.zeros((size, cells), F32))
                pieces.append(jnp.concatenate(lanes, axis=1))
            results.append(along_lat(jnp.concatenate(pieces, axis=0)))
        smooth = along_lon(jnp.concatenate(results, axis=0))
        for l in range(levels):
            block = smooth[l // 2 * size : (l // 2 + 1) * size]
            block = block[:, l % 2 * cells : (l % 2 + 1) * cells].reshape(each, rows, cells)
            extra = jnp.stack(
                [
                    edge[group, l, :, j * cells : (j + 1) * cells]
                    for j in range(spot, spot + each)
                ], axis=0
            )
            out[some, l] = scale * (block + extra)


def divisor(count, limit):
    return max(n for n in range(1, count + 1) if count % n == 0 and (n <= limit or n == 1))


def per_device(
    ensemble,
    static_sigma,
    lat_taps,
    lon_taps,
    step_len,
    send_cols,
    send_count,
    obs_ref,
    obs_level,
    obs_weight,
    innovation,
    obs_precision,
):
    members, levels, rows, cells = ensemble.shape
    half = (lat_taps.shape[0] - 1) // 2
    n_lat, n_lon = lax.axis_size("lat"), lax.axis_size("lon")
    devices = n_lat * n_lon
    slots = send_cols.shape[3]
    scale = HYBRID_ENSEMBLE / math.sqrt(members - 1)

    positions = obs_ref.reshape(obs_ref.shape[2], -1)
    weight = obs_weight.reshape(positions.shape)
    task = levels // n_lat
    each = cells // (2 * half)
    groups = members // each
    assert task * n_lat == levels and each * 2 * half == cells and groups * each == members
    assert levels % each == 0

    wide_slots = max(slots, 256)
    cols = send_cols.reshape(-1, wide_slots)
    iterations = step_len.shape[0]
    some = divisor(each, max(1, 256 // (n_lat * rows)))
    lat_size = n_lat * rows * some
    later = max(1, iterations - 1)
    count_width = -(-devices // 128) * 128
    smem = pl.BlockSpec(memory_space=pltpu.SMEM)
    hbm = pl.BlockSpec(memory_space=pl.ANY)
    exchanges = 4 + iterations + 3 * (iterations - 1)
    strip = (groups, levels, rows, cells)
    narrow = slots % LANES == 0 and levels == 8 and slots // LANES * levels % 16 == 0
    block = (devices, slots // LANES * levels, LANES)
    lat_shape = (2 * each * rows, 3 * each * rows)
    pair_shape = (2, 2 * cells, 2 * cells)
    edge_shape = (2, 2 * cells, each * cells)
    packed = 2 * each
    side_strip = (members // packed, levels, rows, cells)
    side_shape = (2, 2 * cells, packed * cells)
    assert members % packed == 0
    departure, near, near_sides, near_held, lat_adjoint, lon_adjoint, edge_adjoint = pl.pallas_call(
        functools.partial(main_kernel, n_lat, n_lon, iterations, narrow),
        out_shape=(
            jax.ShapeDtypeStruct((1, positions.shape[1]), F32),
            jax.ShapeDtypeStruct((2,) + ensemble.shape, BF16),
            jax.ShapeDtypeStruct((3, 2) + side_strip, BF16),
            jax.ShapeDtypeStruct((3, 3, levels, rows, cells), F32),
            jax.ShapeDtypeStruct(lat_shape, BF16),
            jax.ShapeDtypeStruct(pair_shape, BF16),
            jax.ShapeDtypeStruct(side_shape, BF16),
        ),
        in_specs=[smem] * 4 + [hbm] * 8,
        out_specs=(VMEM, hbm, VMEM, VMEM, VMEM, VMEM, VMEM),
        scratch_shapes=[
            pltpu.VMEM((1, count_width), jnp.int32),
            pltpu.VMEM((devices, 1, count_width), jnp.int32),
            pltpu.VMEM((n_lat, members, task, rows, cells), BF16),
            pltpu.VMEM((2,) + strip, BF16),
            pltpu.VMEM((2,) + side_strip, BF16),
            pltpu.VMEM((2 * n_lat, groups, task, rows, cells), BF16),
            pltpu.VMEM((devices, levels, slots), F32),
            pltpu.VMEM((iterations, devices, levels, slots), F32),
            pltpu.VMEM((levels, rows, cells), F32),
            pltpu.VMEM((later, 3 * n_lat, task, rows, cells), F32),
            pltpu.VMEM((n_lat, task, rows, cells), F32),
            pltpu.VMEM((later, n_lat, task, rows, cells), F32),
            pltpu.VMEM((devices, levels, slots), F32),
            pltpu.VMEM((later, devices, levels, slots), F32),
        ]
        + ([pltpu.VMEM(block, jnp.int16), pltpu.VMEM((exchanges - 4,) + block, jnp.int16)] if narrow else [])
        + [
            pltpu.VMEM(positions.shape, jnp.int32),
            pltpu.VMEM(positions.shape, jnp.int32),
            pltpu.VMEM((2 * lat_size, lat_size), BF16),
            pltpu.VMEM(pair_shape, BF16),
            pltpu.VMEM(edge_shape, BF16),
            pltpu.VMEM((n_lat, groups + 1, task, rows, each * cells), F32),
            pltpu.VMEM(ensemble.shape, BF16),
            pltpu.VMEM((1, devices), jnp.int32),
            pltpu.VMEM(cols.shape, jnp.int32),
            pltpu.VMEM(positions.shape, jnp.int32),
            pltpu.VMEM((1, positions.shape[1]), jnp.int32),
            pltpu.VMEM(positions.shape, F32),
            pltpu.VMEM((1, positions.shape[1]), F32),
            pltpu.VMEM((1, positions.shape[1]), F32),
            pltpu.SemaphoreType.DMA((exchanges,)),
            pltpu.SemaphoreType.DMA((exchanges,)),
            pltpu.SemaphoreType.DMA((2 * n_lat,)),
            pltpu.SemaphoreType.DMA((2 * n_lat,)),
            pltpu.SemaphoreType.DMA((6,)),
            pltpu.SemaphoreType.DMA((6,)),
            pltpu.SemaphoreType.DMA((9,)),
            pltpu.SemaphoreType.DMA((9,)),
            pltpu.SemaphoreType.DMA((8,)),
            pltpu.SemaphoreType.DMA((2,)),
        ],
        compiler_params=pltpu.CompilerParams(
            collective_id=0, has_side_effects=True, vmem_limit_bytes=VMEM_LIMIT
        ),
        name="analysis",
    )(
        static_sigma, step_len, lat_taps, lon_taps, ensemble, send_count.reshape(1, -1), cols,
        positions, obs_level.reshape(1, -1), weight, innovation.reshape(1, -1),
        obs_precision.reshape(1, -1),
    )
    batch = packed
    own_spec = pl.BlockSpec((batch, levels, rows, cells), lambda k: (k, 0, 0, 0))
    near_spec = pl.BlockSpec((2, batch, levels, rows, cells), lambda k: (0, k, 0, 0, 0))
    control, static, departure = pl.pallas_call(
        functools.partial(adjoint_kernel, scale, n_lat),
        grid=(members // batch,),
        out_shape=(
            jax.ShapeDtypeStruct(ensemble.shape, F32),
            jax.ShapeDtypeStruct((levels, rows, cells), F32),
            jax.ShapeDtypeStruct(departure.shape, F32),
        ),
        in_specs=[smem, own_spec, near_spec] + [VMEM] * 6,
        out_specs=(
            pl.BlockSpec((batch, levels, rows, cells), lambda k: (k, 0, 0, 0)),
            pl.BlockSpec((levels, rows, cells), lambda k: (0, 0, 0)),
            pl.BlockSpec(departure.shape, lambda k: (0, 0)),
        ),
        scratch_shapes=[
            pltpu.VMEM((3, levels, rows, cells), F32),
            pltpu.VMEM((3, 2, levels, rows, cells), F32),
            pltpu.VMEM((members // packed + 1, levels, rows, packed * cells), F32),
        ],
        compiler_params=pltpu.CompilerParams(vmem_limit_bytes=VMEM_LIMIT),
        name="adjoint",
    )(
        static_sigma, ensemble, near, near_sides, near_held, lon_adjoint, lat_adjoint,
        edge_adjoint, departure,
    )
    return control, static, departure.reshape(1, 1, -1)


def solution(mesh):
    return jax.shard_map(
        per_device,
        mesh=mesh,
        in_specs=(
            P(None, None, "lat", "lon"),
            P(),
            P(),
            P(),
            P(),
            P("lat", "lon", None, None),
            P("lat", "lon", None),
            P("lat", "lon", None, None),
            P("lat", "lon", None),
            P("lat", "lon", None, None),
            P("lat", "lon", None),
            P("lat", "lon", None),
        ),
        out_specs=(P(None, None, "lat", "lon"), P(None, "lat", "lon"), P("lat", "lon", None)),
        check_vma=False,
    )
```

```python
import functools
import math

import jax
import jax.numpy as jnp
from jax import lax
from jax.experimental import pallas as pl
from jax.experimental.pallas import tpu as pltpu
from jax.sharding import PartitionSpec as P

HYBRID_STATIC = 0.5
HYBRID_ENSEMBLE = 0.8660254037844386
BF16 = jnp.bfloat16
F32 = jnp.float32
MESH = pl.DeviceIdType.MESH
LANES = 128
STEPS = 16383.0
VMEM_LIMIT = 60 * 2**20
VMEM = pl.BlockSpec(memory_space=pltpu.VMEM)


def halves(x):
    high = x.astype(BF16)
    return high, (x - high.astype(F32)).astype(BF16)


def dot(a, b):
    return jnp.dot(a, b, preferred_element_type=F32)


def dot_nt(a, b):
    return lax.dot_general(a, b, (((1,), (1,)), ((), ())), preferred_element_type=F32)


def dot3(a, b):
    a_high, a_low = halves(a)
    b_high, b_low = halves(b)
    return dot(a_high, b_high) + dot(a_high, b_low) + dot(a_low, b_high)


def iota(shape, dim):
    return lax.broadcasted_iota(jnp.int32, shape, dim)


def obs_step(table, hi, lo, weight, innov, prec, departure, out, rows, slots):
    chunk = 2048 if rows <= 256 else 256
    points = hi.shape[0]
    if table is not None:
        table_both = jnp.concatenate(halves(table[...].reshape(rows, slots)), axis=0)

    def step(index, carry):
        where = pl.ds(pl.multiple_of(index * chunk, chunk), chunk)
        row_ids = iota((rows, chunk), 0)
        slot_ids = iota((slots, chunk), 0)
        value = -innov[:, where]
        if table is not None:
            for q in range(points):
                lo_hot = jnp.where(slot_ids == lo[q : q + 1, where], 1.0, 0.0).astype(BF16)
                product = dot(table_both, lo_hot)
                product = product[:rows] + product[rows:]
                picked = jnp.sum(
                    jnp.where(row_ids == hi[q : q + 1, where], product, 0.0), axis=0, keepdims=True
                )
                value = value + weight[q : q + 1, where] * picked
            departure[:, where] = value
        value = prec[:, where] * value
        total = None
        for q in range(points):
            lo_hot = jnp.where(slot_ids == lo[q : q + 1, where], 1.0, 0.0).astype(BF16)
            pushed = weight[q : q + 1, where] * value
            high = pushed.astype(BF16).astype(F32)
            chosen = row_ids == hi[q : q + 1, where]
            both = jnp.concatenate(
                [jnp.where(chosen, high, 0.0), jnp.where(chosen, pushed - high, 0.0)], axis=0
            ).astype(BF16)
            term = dot_nt(both, lo_hot)
            term = term[:rows] + term[rows:]
            total = term if total is None else total + term
        return carry + total

    total = lax.fori_loop(0, hi.shape[1] // chunk, step, jnp.zeros((rows, slots), F32))
    out[...] = total.reshape(out.shape)


def encode(values, out):
    devices, levels, slots = values.shape
    lane = iota((devices, levels, LANES), 2)
    codes = []
    for first in range(0, slots, LANES):
        value = values[:, :, first : first + LANES]
        top = jnp.max(jnp.abs(value), axis=2, keepdims=True)
        power = jnp.clip(jnp.ceil(jnp.log2(jnp.maximum(top, 1e-30))), -99.0, 120.0)
        value = jnp.clip(jnp.floor(value * (STEPS * jnp.exp2(-power)) + 0.5), -STEPS, STEPS)
        shift = jnp.broadcast_to(power.astype(jnp.int32) + 128, lane.shape)
        bit = jnp.bitwise_and(jnp.right_shift(shift, jnp.bitwise_and(lane, 7)), 1)
        codes.append(2 * value.astype(jnp.int32) + bit)
    out[...] = jnp.concatenate(codes, axis=1).astype(jnp.int16)


def decode(coded, out):
    devices, levels, slots = out.shape
    code = coded[...].astype(jnp.int32)
    for piece in range(slots // LANES):
        some = code[:, piece * levels : (piece + 1) * levels]
        bit = jnp.bitwise_and(some, 1).astype(F32).reshape(devices * levels, LANES)
        row = iota((LANES, LANES), 0)
        worth = jnp.where(row < 8, jnp.exp2(row.astype(F32)), 0.0).astype(BF16)
        power = dot(bit.astype(BF16), worth).reshape(some.shape) - 128.0
        value = jnp.right_shift(some, 1).astype(F32) * (jnp.exp2(power) * (1.0 / STEPS))
        out[:, :, piece * LANES : (piece + 1) * LANES] = value


def cell_and_row(col, cells):
    if cells & (cells - 1):
        return col % cells, col // cells
    return jnp.bitwise_and(col, cells - 1), jnp.right_shift(col, cells.bit_length() - 1)


def split(ids, size):
    inner, outer = cell_and_row(ids, size)
    return outer, inner


def to_slots(cols, field, out):
    levels, lat_rows, cells = field.shape
    slots = out.shape[2]
    width = cols.shape[1]
    per_row = width // slots
    rows = jnp.concatenate([field[:, r, :] for r in range(lat_rows)], axis=0)
    count = rows.shape[0]
    both = jnp.concatenate(halves(rows), axis=0)

    def step(index, carry):
        col = cols[pl.ds(index, 1), :]
        cell, at_row = cell_and_row(col, cells)
        cell_hot = jnp.where(iota((cells, width), 0) == cell, 1.0, 0.0).astype(BF16)
        product = dot(both, cell_hot)
        product = product[:count] + product[count:]
        row = jnp.broadcast_to(at_row, (levels, width))
        total = jnp.zeros((levels, width), F32)
        for r in range(lat_rows):
            total = jnp.where(row == r, product[r * levels : (r + 1) * levels], total)
        for j in range(per_row):
            out[index * per_row + j] = total[:, j * slots : (j + 1) * slots]
        return carry

    lax.fori_loop(0, cols.shape[0], step, 0, unroll=4)


def to_columns(cols, values, shape):
    levels, lat_rows, cells = shape
    slots = values.shape[2]
    width = cols.shape[1]
    per_row = width // slots
    count = levels * lat_rows

    def step(index, total):
        col = cols[pl.ds(index, 1), :]
        cell, at_row = cell_and_row(col, cells)
        cell_hot = jnp.where(iota((cells, width), 0) == cell, 1.0, 0.0).astype(BF16)
        chosen = iota((lat_rows, width), 0) == at_row
        value = values[index * per_row]
        if per_row > 1:
            value = jnp.concatenate(
                [values[index * per_row + j] for j in range(per_row)], axis=1
            )
        high = value.astype(BF16).astype(F32)
        low = value - high
        parts = [jnp.where(chosen, high[l : l + 1], 0.0) for l in range(levels)]
        parts += [jnp.where(chosen, low[l : l + 1], 0.0) for l in range(levels)]
        return total + dot_nt(jnp.concatenate(parts, axis=0).astype(BF16), cell_hot)

    total = lax.fori_loop(
        0, cols.shape[0], step, jnp.zeros((2 * count, cells), F32), unroll=4
    )
    return (total[:count] + total[count:]).reshape(shape)


def pick(width, group, side, cells):
    row, col = iota((cells, cells), 0), iota((cells, cells), 1)
    member, spot = split(col, width)
    here = row == (spot if side else spot + (cells - width))
    if group is not None:
        here = jnp.logical_and(here, member == group)
    return jnp.where(here, 1.0, 0.0).astype(BF16)


def make_strips(ens, strips):
    _, groups, levels, rows, cells = strips.shape
    each = ens.shape[0] // groups
    width = cells // each
    total = None
    for j in range(each):
        some = jnp.concatenate([ens[g * each + j] for g in range(groups)], axis=0)
        some = some.reshape(groups * levels * rows, cells)
        both = jnp.concatenate([pick(width, j, 0, cells), pick(width, j, 1, cells)], axis=1)
        term = dot(some, both)
        total = term if total is None else total + term
    for side in range(2):
        strips[side] = (
            total[:, side * cells : (side + 1) * cells].astype(BF16).reshape(strips.shape[1:])
        )


def covariance(ens_coef, static_coef, whole, strips, field, lat_op, lon_op, edge_op, edge, out, first, arrive):
    n_lat, members, levels, rows, cells = whole.shape
    groups = strips.shape[2]
    each = members // groups
    some = lat_op.shape[1] // (n_lat * rows)
    parts = each // some
    size = n_lat * some * rows
    width = cells // each
    edge_high, edge_low = edge_op[0], edge_op[1]
    sides = []
    for side in range(2):
        block = field[2 * side * n_lat : (2 * side + 1) * n_lat]
        high, low = halves(block.reshape(n_lat * levels * rows, cells))
        tile = pick(width, None, side, cells)
        sides.append((dot(high, tile) + dot(low, tile)).reshape(n_lat, levels, rows, cells))
    for a in range(n_lat):
        wide = []
        for side in range(2):
            h = sides[side][a]
            terms = (strips[side, a].astype(F32) * h[None]).reshape(groups * levels * rows, cells)
            wide.append(jnp.concatenate([terms, h.reshape(levels * rows, cells)], axis=0))
        high, low = halves(jnp.concatenate(wide, axis=1))
        edge[a] = (
            dot(high, edge_high) + dot(high, edge_low) + dot(low, edge_high)
        ).reshape(edge.shape[1:])
    lon_high, lon_low = lon_op[0], lon_op[1]

    def smooth(pieces, group, width_of):
        lanes = []
        for index, (l, p, piece) in enumerate(pieces):
            lanes.append(piece.reshape(size, cells))
        count = len(lanes)
        if count % 2:
            lanes.append(jnp.zeros((size, cells), F32))
        results = []
        for first in range(0, count, 2):
            high, low = halves(jnp.concatenate(lanes[first : first + 2], axis=1))
            mid = dot(high, lon_high) + dot(high, lon_low) + dot(low, lon_high)
            extra = []
            for l, p, piece in pieces[first : first + 2]:
                at = [width_of(p * some + j) for j in range(some)]
                extra.append(
                    jnp.stack(
                        [edge[:, group, l, :, x * cells : (x + 1) * cells] for x in at], axis=1
                    ).reshape(size, cells)
                )
            if len(extra) == 1:
                extra.append(jnp.zeros((size, cells), F32))
            high, low = halves(mid + jnp.concatenate(extra, axis=1))
            both = dot(lat_op[...], high)
            done = both[:size] + both[size:] + dot(lat_op[:size], low)
            for index in range(min(2, count - first)):
                results.append(
                    done[:, index * cells : (index + 1) * cells].reshape(n_lat, some, rows, cells)
                )
        return results

    own = [field[n_lat : 2 * n_lat, l] for l in range(levels)]

    def step(group, total):
        pieces, kept = [], []
        for l in range(levels):
            for p in range(parts):
                values = whole[:, pl.ds(group * each + p * some, some), l].astype(F32)
                kept.append((l, values))
                pieces.append((l, p, values * own[l][:, None]))
        done = smooth(pieces, group, lambda x: x)
        total = list(total)
        for (l, values), result in zip(kept, done):
            total[l] = total[l] + jnp.sum(values * result, axis=1)
        return tuple(total)

    zero = jnp.zeros((n_lat, rows, cells), F32)
    total = lax.fori_loop(0, first, step, (zero,) * levels)
    if arrive is not None:
        arrive()
    total = lax.fori_loop(first, groups, step, total)
    pieces = []
    for l in range(levels):
        piece = [own[l]] + [zero] * (some - 1)
        pieces.append((l, 0, jnp.stack(piece, axis=1)))
    done = smooth(pieces, groups, lambda x: 0)
    for l in range(levels):
        out[:, l] = ens_coef * total[l] + static_coef[l] * done[l][:, 0]


def banded(taps, offset):
    total = jnp.zeros(offset.shape, F32)
    for t in range(len(taps)):
        total = jnp.where(offset == t, taps[t], total)
    return total


def store_halves(ref, value):
    ref[0], ref[1] = halves(value)


def edge_operator(taps, reach, each, cells, op):
    width = cells // each
    row, col = iota((2 * cells, cells), 0), iota((2 * cells, cells), 1)
    side, lane = split(row, cells)
    member, spot = split(lane, width)
    at = jnp.where(side == 0, spot - width, spot + cells)
    value = banded(taps, at - col + reach)
    for j in range(each):
        high, low = halves(jnp.where(member == j, value, 0.0))
        op[0, :, j * cells : (j + 1) * cells] = high
        op[1, :, j * cells : (j + 1) * cells] = low


def pair_operator(taps, reach, cells, op):
    row, col = iota((2 * cells, 2 * cells), 0), iota((2 * cells, 2 * cells), 1)
    row_block, row_at = split(row, cells)
    col_block, col_at = split(col, cells)
    store_halves(
        op, jnp.where(row_block == col_block, banded(taps, row_at - col_at + reach), 0.0)
    )


def make_operators(n_lat, rows, cells, each, lat_taps, lon_taps, lat_op, lon_op, edge_op):
    count = lat_taps.shape[0]
    half = (count - 1) // 2
    lat = [lat_taps[t] for t in range(count)]
    lon = [lon_taps[t] for t in range(count)]
    size = lat_op.shape[1]
    some = size // (n_lat * rows)
    row, col = iota((size, size), 0), iota((size, size), 1)

    def lat_of(ids):
        outer, r = split(ids, rows)
        a, j = split(outer, some)
        return a * rows + r, j

    row_at, row_member = lat_of(row)
    col_at, col_member = lat_of(col)
    high, low = halves(
        jnp.where(row_member == col_member, banded(lat, col_at - row_at + half), 0.0)
    )
    lat_op[:size], lat_op[size:] = halves(
        dot_nt(high, high) + dot_nt(high, low) + dot_nt(low, high)
    )
    corr = []
    for lag in range(-2 * half, 2 * half + 1):
        terms = [lon[t] * lon[t - lag] for t in range(count) if 0 <= t - lag < count]
        corr.append(functools.reduce(lambda a, b: a + b, terms))
    pair_operator(corr, 2 * half, cells, lon_op)
    edge_operator(corr, 2 * half, each, cells, edge_op)


def make_adjoint_operators(rows, each, packed, cells, lat_taps, lon_taps, lat_op, lon_op, edge_op):
    count = lat_taps.shape[0]
    half = (count - 1) // 2
    lat = [lat_taps[t] for t in range(count)][::-1]
    lon = [lon_taps[t] for t in range(count)][::-1]
    shape = (each * rows, 3 * each * rows)
    row_member, row_at = split(iota(shape, 0), rows)
    outer, col_at = split(iota(shape, 1), rows)
    part, col_member = split(outer, each)
    offset = (part - 1) * rows + col_at - row_at + half
    lat_op[: shape[0]], lat_op[shape[0] :] = halves(
        jnp.where(row_member == col_member, banded(lat, offset), 0.0)
    )
    pair_operator(lon, half, cells, lon_op)
    edge_operator(lon, half, packed, cells, edge_op)


def main_kernel(n_lat, n_lon, iterations, narrow, *refs):
    if not narrow:
        at = 33
        refs = refs[:at] + (None, None) + refs[at:]
    main_body(n_lat, n_lon, iterations, *refs)


def main_body(
    n_lat, n_lon, iterations,
    sigma, step, lat_taps, lon_taps, ens_far, count_far, cols_far, pos_far, level_far, weight_far,
    innov_far, prec_far,
    departure, near, near_sides, near_held, lat_adjoint, lon_adjoint, edge_adjoint,
    count_row, counts, whole, strips, side_strips, near_strips, pushed, incoming, held, field, part, part_in,
    packed, table, coded, arrived, hi, lo, lat_op, lon_op, edge_op, edge,
    ens, send_count, cols, pos, level, weight, innov, prec,
    ex_send, ex_recv, near_send, near_recv, side_send, side_recv, held_send, held_recv, load_sem, own_sem,
):
    lat_at, lon_at = lax.axis_index("lat"), lax.axis_index("lon")
    me = lat_at * n_lon + lon_at
    devices = n_lat * n_lon
    levels, rows, cells = held.shape
    slots = pushed.shape[2]
    members = ens.shape[0]
    task = levels // n_lat
    each = members // strips.shape[1]

    def place(d):
        return (d // n_lon, d % n_lon)

    barrier = pltpu.get_barrier_semaphore()

    def greet(k, carry):
        pl.semaphore_signal(
            barrier, inc=1, device_id=place((me + k) % devices), device_id_type=MESH
        )
        return carry

    lax.fori_loop(1, devices, greet, 0)
    loads = [
        pltpu.make_async_copy(far, here, load_sem.at[index])
        for index, (far, here) in enumerate(
            (
                (count_far, send_count), (ens_far, ens), (pos_far, pos), (level_far, level),
                (weight_far, weight), (innov_far, innov), (prec_far, prec), (cols_far, cols),
            )
        )
    ]
    for load in loads:
        load.start()
    count_row[...] = jnp.zeros_like(count_row)
    loads[0].wait()
    count_row[:, :devices] = send_count[...]
    make_operators(n_lat, rows, cells, each, lat_taps, lon_taps, lat_op, lon_op, edge_op)
    pl.semaphore_wait(barrier, devices - 1)

    def copy_to(source, target, number, device):
        return pltpu.make_async_remote_copy(
            src_ref=source, dst_ref=target, send_sem=ex_send.at[number],
            recv_sem=ex_recv.at[number], device_id=device, device_id_type=MESH,
        )

    def send(source, target, number):
        def one(k, carry):
            d = (me + k) % devices
            copy_to(source(d), target.at[me], number, place(d)).start()
            return carry

        lax.fori_loop(1, devices, one, 0)

    def wait(target, number, count=devices - 1):
        every = target.at[pl.ds(0, count)]
        copy = copy_to(every, every, number, place((me + 1) % devices))
        copy.wait_send()
        copy.wait_recv()

    def exchange(values, target, number, meanwhile=None):
        if coded is None:
            send(lambda d: values.at[d], target, number)
            target[me] = values[me]
        else:
            index = number - 3
            encode(values, coded)
            send(lambda d: coded.at[d], arrived.at[index], number)
            arrived[index, me] = coded[me]
        if meanwhile is not None:
            meanwhile()
        if coded is None:
            wait(target, number)
        else:
            wait(arrived.at[index], number)
            decode(arrived.at[index], target)

    def of_task(a):
        return pl.ds(a * task, task)

    def lat_peer(k):
        return (lat_at + k) % n_lat

    def lon_peer(turn):
        return (lon_at + turn + n_lon) % n_lon

    send(lambda d: count_row, counts, 0)
    counts[me] = count_row[...]
    early = strips.shape[1] * 1 // 2 * each
    halves_of = (pl.ds(0, early), pl.ds(early, members - early))

    def spread(index):
        some = halves_of[index]
        for k in range(1, n_lat):
            a = lat_peer(k)
            copy_to(
                ens_far.at[some, of_task(a)], whole.at[lat_at, some],
                ex_send.shape[0] - 1 if index else 1, (a, lon_at),
            ).start()

    def spread_wait(index):
        every = whole.at[pl.ds(0, n_lat - 1), halves_of[index]]
        copy = copy_to(
            every, every, ex_send.shape[0] - 1 if index else 1, place((me + 1) % devices)
        )
        copy.wait_send()
        copy.wait_recv()

    spread(0)
    loads[1].wait()
    whole[lat_at] = ens[:, of_task(lat_at)]
    make_strips(ens, strips)
    for k in range(n_lat):
        a = lat_peer(k)
        for side, turn in enumerate((1, -1)):
            copy_to(
                strips.at[side, :, of_task(a)], near_strips.at[side * n_lat + lat_at], 2,
                (a, lon_peer(turn)),
            ).start()
    for load in loads[2:]:
        load.wait()
    wait(counts, 0)
    received = jnp.concatenate([counts[d] for d in range(devices)], axis=0)
    width = received.shape[1]
    column = jnp.sum(
        jnp.where(iota((devices, width), 1) == me, received, 0), axis=1, keepdims=True
    )
    as_row = jnp.sum(
        jnp.where(iota((devices, width), 0) == iota((devices, width), 1), column, 0),
        axis=0, keepdims=True,
    )
    ends = jnp.sum(
        jnp.where(iota((devices, width), 1) <= iota((devices, width), 0), as_row, 0),
        axis=1, keepdims=True,
    )
    for q in range(pos.shape[0]):
        place_q = pos[q : q + 1, :]
        past = place_q >= ends
        source = jnp.sum(jnp.where(past, 1, 0), axis=0, keepdims=True)
        lo[q : q + 1, :] = place_q - jnp.sum(jnp.where(past, column, 0), axis=0, keepdims=True)
        hi[q : q + 1, :] = source * levels + level[...]

    def near_chunk(chunk, begin):
        for index, turn in enumerate((1, -1)):
            some = of_task((lat_at + turn + chunk + n_lat) % n_lat)
            mine = of_task((lat_at + chunk) % n_lat)
            has_send, has_recv = lat_has(n_lat, lat_at, turn)
            if chunk == 0:
                local = pltpu.make_async_copy(
                    whole.at[(lat_at - turn + n_lat) % n_lat], near.at[index, :, mine],
                    own_sem.at[index],
                )
                pl.when(has_recv)(local.start if begin else local.wait)
                continue
            number = index * n_lat + chunk
            if begin:
                sent = pltpu.make_async_remote_copy(
                    src_ref=ens_far.at[:, some], dst_ref=near.at[index, :, some],
                    send_sem=near_send.at[number], recv_sem=near_recv.at[number],
                    device_id=((lat_at + turn + n_lat) % n_lat, lon_at), device_id_type=MESH,
                )
                pl.when(has_send)(sent.start)
            else:
                sent = pltpu.make_async_remote_copy(
                    src_ref=ens_far.at[:, some], dst_ref=near.at[index, :, mine],
                    send_sem=near_send.at[number], recv_sem=near_recv.at[number],
                    device_id=((lat_at + turn + n_lat) % n_lat, lon_at), device_id_type=MESH,
                )
                pl.when(has_send)(sent.wait_send)
                pl.when(has_recv)(sent.wait_recv)

    def side_copies(begin):
        for up, climb in enumerate((1, 0, -1)):
            for side, turn in enumerate((1, -1)):
                exchange_pair(
                    begin, *lat_has(n_lat, lat_at, climb),
                    src_ref=side_strips.at[side],
                    dst_ref=near_sides.at[up, side],
                    send_sem=side_send.at[up * 2 + side], recv_sem=side_recv.at[up * 2 + side],
                    device_id=((lat_at + climb + n_lat) % n_lat, lon_peer(turn)),
                )

    def prepare():
        spread(1)
        make_strips(ens, side_strips)

    number = 3
    for iteration in range(iterations):
        before = iteration - 1
        if iteration > 0:
            around = field.at[before]
            for k in range(n_lat):
                a = lat_peer(k)
                for at, turn in enumerate((1, 0, -1)):
                    if k == 0 and turn == 0:
                        continue
                    copy_to(
                        held.at[of_task(a)], around.at[at * n_lat + lat_at], number,
                        (a, lon_peer(turn)),
                    ).start()
            field[before, n_lat + lat_at] = held[of_task(lat_at)]
            if iteration == 1:
                spread_wait(0)
                wait(near_strips, 2, 2 * n_lat)
            wait(around, number, 3 * n_lat - 1)
            if iteration == 1:
                side_copies(True)
            covariance(
                HYBRID_ENSEMBLE**2 / (members - 1),
                [HYBRID_STATIC**2 * sigma[lat_at * task + l] ** 2 for l in range(task)],
                whole, near_strips.reshape(2, n_lat, *near_strips.shape[1:]), around,
                lat_op, lon_op, edge_op, edge, part, early // each,
                functools.partial(spread_wait, 1) if iteration == 1 else None,
            )
            home = part_in.at[before]
            for k in range(1, n_lat):
                a = lat_peer(k)
                copy_to(part.at[a], home.at[lat_at], number + 1, (a, lon_at)).start()
            part_in[before, lat_at] = part[lat_at]
            if iteration == 1:
                near_chunk(0, True)
                near_chunk(1, True)
            wait(home, number + 1, n_lat - 1)
            if iteration == 1:
                for chunk in range(2, 2 + (n_lat - 2) // 2):
                    near_chunk(chunk, True)
            to_slots(cols, part_in[before].reshape(levels, rows, cells), packed)
            exchange(
                packed, table.at[before], number + 2,
                functools.partial(
                    make_adjoint_operators, rows, each, members // side_strips.shape[1], cells, lat_taps, lon_taps,
                    lat_adjoint, lon_adjoint, edge_adjoint,
                ) if iteration == 1 else None,
            )
            number += 3
            if iteration == 1:
                for chunk in range(2 + (n_lat - 2) // 2, n_lat):
                    near_chunk(chunk, True)
        obs_step(
            table.at[before] if iteration > 0 else None,
            hi, lo, weight, innov, prec, departure, pushed, devices * levels, slots,
        )
        exchange(
            pushed, incoming.at[iteration], number,
            prepare if iteration == 0 else None,
        )
        number += 1
        forcing = to_columns(cols, incoming.at[iteration], held.shape)
        if iteration == 0:
            held[...] = -step[0] * forcing
        else:
            held[...] = held[...] - step[iteration] * (forcing + held[...])

    held_copies(n_lat, n_lon, lat_at, lon_at, held, near_held, held_send, held_recv, True)
    near_held[1, 1] = held[...]
    for chunk in range(n_lat):
        near_chunk(chunk, False)
    side_copies(False)
    held_copies(n_lat, n_lon, lat_at, lon_at, held, near_held, held_send, held_recv, False)


def exchange_pair(begin, has_send, has_recv, **copy):
    made = pltpu.make_async_remote_copy(device_id_type=MESH, **copy)
    if begin:
        pl.when(has_send)(made.start)
    else:
        pl.when(has_send)(made.wait_send)
        pl.when(has_recv)(made.wait_recv)


def lat_has(n_lat, lat_at, step):
    send = jnp.logical_and(lat_at + step >= 0, lat_at + step < n_lat)
    recv = jnp.logical_and(lat_at - step >= 0, lat_at - step < n_lat)
    return send, recv


def held_copies(n_lat, n_lon, lat_at, lon_at, held, near_held, held_send, held_recv, begin):
    for up, step in enumerate((1, 0, -1)):
        has = lat_has(n_lat, lat_at, step)
        for side, turn in enumerate((1, 0, -1)):
            if step == 0 and turn == 0:
                continue
            exchange_pair(
                begin, *has,
                src_ref=held, dst_ref=near_held.at[up, side],
                send_sem=held_send.at[up * 3 + side], recv_sem=held_recv.at[up * 3 + side],
                device_id=((lat_at + step + n_lat) % n_lat, (lon_at + turn + n_lon) % n_lon),
            )


def adjoint_kernel(
    scale, n_lat,
    sigma, members, near, sides, field, lon_op, lat_op, edge_op, departure,
    out, static_out, departure_out,
    own, edge_field, edge,
):
    batch, levels, rows, cells = out.shape
    groups = sides.shape[2]
    each = lat_op.shape[0] // (2 * rows)
    packed = edge_op.shape[2] // cells
    width = cells // packed
    lat_at = lax.axis_index("lat")
    keep = (lat_at > 0, None, lat_at < n_lat - 1)
    lon_high, lon_low = lon_op[0], lon_op[1]
    size = lat_op.shape[0] // 2

    def kept(part, value):
        return value if keep[part] is None else jnp.where(keep[part], value, 0.0)

    def along_lat(stacked):
        high, low = halves(stacked)
        both = dot(lat_op[...], high)
        return both[:size] + both[size:] + dot(lat_op[:size], low)

    def along_lon(stacked):
        high, low = halves(stacked)
        return dot(high, lon_high) + dot(high, lon_low) + dot(low, lon_high)

    @pl.when(pl.program_id(0) == 0)
    def _():
        departure_out[...] = departure[...]
        for part in range(3):
            own[part] = kept(part, field[part, 1])
            for side in range(2):
                value = kept(part, field[part, 2 * side]).reshape(levels * rows, cells)
                high, low = halves(value)
                tile = pick(width, None, side, cells)
                edge_field[part, side] = (dot(high, tile) + dot(low, tile)).reshape(
                    levels, rows, cells
                )

        def edge_of(group):
            results = []
            for first in range(0, levels, each):
                pieces = []
                for part in range(3):
                    lanes = []
                    for side in range(2):
                        value = edge_field[part, side, first : first + each]
                        if group is not None:
                            some = sides[part, side, group, first : first + each].astype(F32)
                            value = kept(part, some * value)
                        lanes.append(value.reshape(size, cells))
                    pieces.append(jnp.concatenate(lanes, axis=1))
                results.append(along_lat(jnp.concatenate(pieces, axis=0)))
            return results

        stacked = jnp.concatenate(
            [piece for g in list(range(groups)) + [None] for piece in edge_of(g)], axis=0
        )
        high, low = halves(stacked)
        edge[...] = (
            dot(high, edge_op[0]) + dot(high, edge_op[1]) + dot(low, edge_op[0])
        ).reshape(edge.shape)
        results = []
        for first in range(0, levels, each):
            stacked = jnp.concatenate(
                [own[part, first : first + each].reshape(size, cells) for part in range(3)], axis=0
            )
            both = jnp.concatenate([stacked, jnp.zeros_like(stacked)], axis=1)
            results.append(along_lat(both))
        smooth = along_lon(jnp.concatenate(results, axis=0))[:, :cells].reshape(
            levels, rows, cells
        )
        for l in range(levels):
            static_out[l] = (HYBRID_STATIC * sigma[l]) * (
                smooth[l] + edge[groups, l, :, :cells]
            )

    for g in range(batch // each):
        some = pl.ds(g * each, each)
        group = pl.program_id(0) * (batch // packed) + g * each // packed
        spot = g * each % packed
        results = []
        for first in range(0, levels, 2):
            pieces = []
            for part in range(3):
                lanes = []
                for l in range(first, min(first + 2, levels)):
                    values = members[some, l] if part == 1 else near[part // 2, some, l]
                    lanes.append(
                        kept(part, values.astype(F32) * own[part, l][None]).reshape(size, cells)
                    )
                if len(lanes) == 1:
                    lanes.append(jnp.zeros((size, cells), F32))
                pieces.append(jnp.concatenate(lanes, axis=1))
            results.append(along_lat(jnp.concatenate(pieces, axis=0)))
        smooth = along_lon(jnp.concatenate(results, axis=0))
        for l in range(levels):
            block = smooth[l // 2 * size : (l // 2 + 1) * size]
            block = block[:, l % 2 * cells : (l % 2 + 1) * cells].reshape(each, rows, cells)
            extra = jnp.stack(
                [
                    edge[group, l, :, j * cells : (j + 1) * cells]
                    for j in range(spot, spot + each)
                ], axis=0
            )
            out[some, l] = scale * (block + extra)


def divisor(count, limit):
    return max(n for n in range(1, count + 1) if count % n == 0 and (n <= limit or n == 1))


def per_device(
    ensemble,
    static_sigma,
    lat_taps,
    lon_taps,
    step_len,
    send_cols,
    send_count,
    obs_ref,
    obs_level,
    obs_weight,
    innovation,
    obs_precision,
):
    members, levels, rows, cells = ensemble.shape
    half = (lat_taps.shape[0] - 1) // 2
    n_lat, n_lon = lax.axis_size("lat"), lax.axis_size("lon")
    devices = n_lat * n_lon
    slots = send_cols.shape[3]
    scale = HYBRID_ENSEMBLE / math.sqrt(members - 1)

    positions = obs_ref.reshape(obs_ref.shape[2], -1)
    weight = obs_weight.reshape(positions.shape)
    task = levels // n_lat
    each = cells // (2 * half)
    groups = members // each
    assert task * n_lat == levels and each * 2 * half == cells and groups * each == members
    assert levels % each == 0

    wide_slots = max(slots, 256)
    cols = send_cols.reshape(-1, wide_slots)
    iterations = step_len.shape[0]
    some = divisor(each, max(1, 256 // (n_lat * rows)))
    lat_size = n_lat * rows * some
    later = max(1, iterations - 1)
    count_width = -(-devices // 128) * 128
    smem = pl.BlockSpec(memory_space=pltpu.SMEM)
    hbm = pl.BlockSpec(memory_space=pl.ANY)
    exchanges = 4 + iterations + 3 * (iterations - 1)
    strip = (groups, levels, rows, cells)
    narrow = slots % LANES == 0 and levels == 8 and slots // LANES * levels % 16 == 0
    block = (devices, slots // LANES * levels, LANES)
    lat_shape = (2 * each * rows, 3 * each * rows)
    pair_shape = (2, 2 * cells, 2 * cells)
    edge_shape = (2, 2 * cells, each * cells)
    packed = 2 * each
    side_strip = (members // packed, levels, rows, cells)
    side_shape = (2, 2 * cells, packed * cells)
    assert members % packed == 0
    departure, near, near_sides, near_held, lat_adjoint, lon_adjoint, edge_adjoint = pl.pallas_call(
        functools.partial(main_kernel, n_lat, n_lon, iterations, narrow),
        out_shape=(
            jax.ShapeDtypeStruct((1, positions.shape[1]), F32),
            jax.ShapeDtypeStruct((2,) + ensemble.shape, BF16),
            jax.ShapeDtypeStruct((3, 2) + side_strip, BF16),
            jax.ShapeDtypeStruct((3, 3, levels, rows, cells), F32),
            jax.ShapeDtypeStruct(lat_shape, BF16),
            jax.ShapeDtypeStruct(pair_shape, BF16),
            jax.ShapeDtypeStruct(side_shape, BF16),
        ),
        in_specs=[smem] * 4 + [hbm] * 8,
        out_specs=(VMEM, hbm, VMEM, VMEM, VMEM, VMEM, VMEM),
        scratch_shapes=[
            pltpu.VMEM((1, count_width), jnp.int32),
            pltpu.VMEM((devices, 1, count_width), jnp.int32),
            pltpu.VMEM((n_lat, members, task, rows, cells), BF16),
            pltpu.VMEM((2,) + strip, BF16),
            pltpu.VMEM((2,) + side_strip, BF16),
            pltpu.VMEM((2 * n_lat, groups, task, rows, cells), BF16),
            pltpu.VMEM((devices, levels, slots), F32),
            pltpu.VMEM((iterations, devices, levels, slots), F32),
            pltpu.VMEM((levels, rows, cells), F32),
            pltpu.VMEM((later, 3 * n_lat, task, rows, cells), F32),
            pltpu.VMEM((n_lat, task, rows, cells), F32),
            pltpu.VMEM((later, n_lat, task, rows, cells), F32),
            pltpu.VMEM((devices, levels, slots), F32),
            pltpu.VMEM((later, devices, levels, slots), F32),
        ]
        + ([pltpu.VMEM(block, jnp.int16), pltpu.VMEM((exchanges - 4,) + block, jnp.int16)] if narrow else [])
        + [
            pltpu.VMEM(positions.shape, jnp.int32),
            pltpu.VMEM(positions.shape, jnp.int32),
            pltpu.VMEM((2 * lat_size, lat_size), BF16),
            pltpu.VMEM(pair_shape, BF16),
            pltpu.VMEM(edge_shape, BF16),
            pltpu.VMEM((n_lat, groups + 1, task, rows, each * cells), F32),
            pltpu.VMEM(ensemble.shape, BF16),
            pltpu.VMEM((1, devices), jnp.int32),
            pltpu.VMEM(cols.shape, jnp.int32),
            pltpu.VMEM(positions.shape, jnp.int32),
            pltpu.VMEM((1, positions.shape[1]), jnp.int32),
            pltpu.VMEM(positions.shape, F32),
            pltpu.VMEM((1, positions.shape[1]), F32),
            pltpu.VMEM((1, positions.shape[1]), F32),
            pltpu.SemaphoreType.DMA((exchanges,)),
            pltpu.SemaphoreType.DMA((exchanges,)),
            pltpu.SemaphoreType.DMA((2 * n_lat,)),
            pltpu.SemaphoreType.DMA((2 * n_lat,)),
            pltpu.SemaphoreType.DMA((6,)),
            pltpu.SemaphoreType.DMA((6,)),
            pltpu.SemaphoreType.DMA((9,)),
            pltpu.SemaphoreType.DMA((9,)),
            pltpu.SemaphoreType.DMA((8,)),
            pltpu.SemaphoreType.DMA((2,)),
        ],
        compiler_params=pltpu.CompilerParams(
            collective_id=0, has_side_effects=True, vmem_limit_bytes=VMEM_LIMIT
        ),
        name="analysis",
    )(
        static_sigma, step_len, lat_taps, lon_taps, ensemble, send_count.reshape(1, -1), cols,
        positions, obs_level.reshape(1, -1), weight, innovation.reshape(1, -1),
        obs_precision.reshape(1, -1),
    )
    batch = packed
    own_spec = pl.BlockSpec((batch, levels, rows, cells), lambda k: (k, 0, 0, 0))
    near_spec = pl.BlockSpec((2, batch, levels, rows, cells), lambda k: (0, k, 0, 0, 0))
    control, static, departure = pl.pallas_call(
        functools.partial(adjoint_kernel, scale, n_lat),
        grid=(members // batch,),
        out_shape=(
            jax.ShapeDtypeStruct(ensemble.shape, F32),
            jax.ShapeDtypeStruct((levels, rows, cells), F32),
            jax.ShapeDtypeStruct(departure.shape, F32),
        ),
        in_specs=[smem, own_spec, near_spec] + [VMEM] * 6,
        out_specs=(
            pl.BlockSpec((batch, levels, rows, cells), lambda k: (k, 0, 0, 0)),
            pl.BlockSpec((levels, rows, cells), lambda k: (0, 0, 0)),
            pl.BlockSpec(departure.shape, lambda k: (0, 0)),
        ),
        scratch_shapes=[
            pltpu.VMEM((3, levels, rows, cells), F32),
            pltpu.VMEM((3, 2, levels, rows, cells), F32),
            pltpu.VMEM((members // packed + 1, levels, rows, packed * cells), F32),
        ],
        compiler_params=pltpu.CompilerParams(vmem_limit_bytes=VMEM_LIMIT),
        name="adjoint",
    )(
        static_sigma, ensemble, near, near_sides, near_held, lon_adjoint, lat_adjoint,
        edge_adjoint, departure,
    )
    return control, static, departure.reshape(1, 1, -1)


def solution(mesh):
    return jax.shard_map(
        per_device,
        mesh=mesh,
        in_specs=(
            P(None, None, "lat", "lon"),
            P(),
            P(),
            P(),
            P(),
            P("lat", "lon", None, None),
            P("lat", "lon", None),
            P("lat", "lon", None, None),
            P("lat", "lon", None),
            P("lat", "lon", None, None),
            P("lat", "lon", None),
            P("lat", "lon", None),
        ),
        out_specs=(P(None, None, "lat", "lon"), P(None, "lat", "lon"), P("lat", "lon", None)),
        check_vma=False,
    )
```
